128 devices in a mesh: sx: 8 (over z, core), sy: 16 (over x, y).
Axes of the slice: x: 4, y: 4, z: 4, core: 2. Of those that a mesh axis runs over, the one named last changes fastest.
Arguments:
- fine_matrix: bfloat16 [16, 32, 2, 7, 64, 64], P('sx', 'sy'), may hold values from -0.75 to 0.75
- prolongator: bfloat16 [16, 32, 2, 7, 64, 64], P('sx', 'sy'), may hold values from -2.5 to 2.5
- aggregate: int32 [16, 32, 2], P('sx', 'sy'), may hold values from 0 to 127, as said below
- face_links: int32 [16, 32, 2, 6], P('sx', 'sy'), may hold values from 0 to 1, as said below
Outputs:
- coarse: bfloat16 [8, 16, 7, 7, 64, 64], P('sx', 'sy')
The draws below stay inside these ranges and needn't reach their ends.
Inputs may be any that keep to these rules, and one draw needn't show every extreme that they name: aggregate[i] is the id bx 16 + by of a box of 2 x 2 x 2 elements: the box that holds element i, or the box beside it across a box face on which element i lies (faces along x or y). face_links[i, f] is the same on both sides of a face, and 0 on the outer faces of the grid.
All inputs are finite; a program needn't handle non-finite values.
Results may differ from the reference program's by a relative error of at most 0.007.
Values may be sent and summed in bfloat16 or wider, within the bound.
A program may use at most 320 MiB of HBM per device.

```python
import jax
import jax.numpy as jnp
from jax import lax

B = 64
CB = 64
NX = 16
NY = 32
BOXES_X = 8
BOXES_Y = 16


def draw_face_links(key, part):
    key_x, key_y, key_z = jax.random.split(key, 3)
    link_x = (jax.random.randint(key_x, (NX - 1, NY, 2), 0, 20) < 17).astype(jnp.int32)
    link_y = (jax.random.randint(key_y, (NX, NY - 1, 2), 0, 20) < 17).astype(jnp.int32)
    link_z = (jax.random.randint(key_z, (NX, NY, 1), 0, 20) < 17).astype(jnp.int32)
    empty_x = jnp.zeros((1, NY, 2), jnp.int32)
    empty_y = jnp.zeros((NX, 1, 2), jnp.int32)
    empty_z = jnp.zeros((NX, NY, 1), jnp.int32)
    minus_x = jnp.concatenate([empty_x, link_x], axis=0)
    plus_x = jnp.concatenate([link_x, empty_x], axis=0)
    minus_y = jnp.concatenate([empty_y, link_y], axis=1)
    plus_y = jnp.concatenate([link_y, empty_y], axis=1)
    minus_z = jnp.concatenate([empty_z, link_z], axis=2)
    plus_z = jnp.concatenate([link_z, empty_z], axis=2)
    return jnp.stack([minus_x, plus_x, minus_y, plus_y, minus_z, plus_z], axis=-1)


def draw_aggregate(key, part):
    picked = jax.random.randint(key, (NX, NY, 2), 0, 8)
    row_x = jnp.arange(NX, dtype=jnp.int32)[:, None, None]
    row_y = jnp.arange(NY, dtype=jnp.int32)[None, :, None]
    box_x = row_x // 2
    box_y = row_y // 2
    step_x = jnp.where((picked == 4) & (row_x % 2 == 0) & (box_x > 0), -1, 0) + jnp.where((picked == 5) & (row_x % 2 == 1) & (box_x < BOXES_X - 1), 1, 0)
    step_y = jnp.where((picked == 6) & (row_y % 2 == 0) & (box_y > 0), -1, 0) + jnp.where((picked == 7) & (row_y % 2 == 1) & (box_y < BOXES_Y - 1), 1, 0)
    return ((box_x + step_x) * BOXES_Y + box_y + step_y).astype(jnp.int32)


def block_levels(own_key, shape, cuts, smallest, largest):
    factor_of = 1.0
    for position, blocks in cuts:
        draws = jax.random.uniform(jax.random.fold_in(jax.random.fold_in(own_key, 6), position), (blocks,), jnp.float32, smallest / len(cuts), largest / len(cuts))
        factor_of = factor_of * jnp.repeat(jnp.exp(draws), shape[position] // blocks).reshape((-1,) + (1,) * (len(shape) - 1 - position))
    return factor_of


def noise(stream_key, shape, scale, limit, cuts=(), held_as=jnp.bfloat16):
    level = block_levels(stream_key, shape, cuts, -0.22, 0.18) if cuts else 1.0
    drawn = jax.random.normal(stream_key, shape, jnp.float32) * scale * level
    return jnp.minimum(jnp.maximum(drawn, -limit), limit).astype(held_as)


def setup_inputs(seed: int = 0) -> dict:
    key_of = jax.random.split(jax.random.key(seed), 5)
    fine_matrix = noise(key_of[0], (NX, NY, 2, 7, B, B), B ** -0.5, 0.75, ((0, 8), (1, 16)))
    prolongator = noise(key_of[1], (NX, NY, 2, 7, B, CB), 0.35, 2.5, ((0, 8), (1, 16)))
    aggregate = draw_aggregate(jax.random.fold_in(key_of[4], 71), 0)
    face_links = draw_face_links(jax.random.fold_in(key_of[4], 71), 0)
    return {"fine_matrix": fine_matrix, "prolongator": prolongator, "aggregate": aggregate, "face_links": face_links}


def neighbour_views(extended):
    padded = jnp.pad(extended, [(0, 0), (0, 0), (1, 1)] + [(0, 0)] * (extended.ndim - 3))
    return [padded[1:-1, 1:-1, 1:3], padded[:-2, 1:-1, 1:3], padded[2:, 1:-1, 1:3],
            padded[1:-1, :-2, 1:3], padded[1:-1, 2:, 1:3], padded[1:-1, 1:-1, 0:2], padded[1:-1, 1:-1, 2:4]]


def slot_ids(aggregate_ext, face_links, first_x, first_y, boxes_y):
    neighbours = jnp.stack(neighbour_views(aggregate_ext), axis=-1)
    count_x, count_y = face_links.shape[0], face_links.shape[1]
    box_x = ((first_x + jnp.arange(count_x, dtype=jnp.int32)) // 2)[:, None, None, None]
    box_y = ((first_y + jnp.arange(count_y, dtype=jnp.int32)) // 2)[None, :, None, None]
    target_x = neighbours // boxes_y
    target_y = neighbours % boxes_y
    within = (target_x - box_x + 1) * 3 + (target_y - box_y + 1)
    present = jnp.concatenate([jnp.ones_like(face_links[..., :1]), face_links], axis=-1) == 1
    return jnp.where(present, within, -1).astype(jnp.int32)


def box_step(direction, parity_x, parity_y):
    shift_x = 0
    shift_y = 0
    if direction == 1 and parity_x == 0:
        shift_x = -1
    if direction == 2 and parity_x == 1:
        shift_x = 1
    if direction == 3 and parity_y == 0:
        shift_y = -1
    if direction == 4 and parity_y == 1:
        shift_y = 1
    return shift_x, shift_y


def image_blocks(fine_matrix, face_links, box_ext):
    views = neighbour_views(box_ext)
    count_x, count_y = fine_matrix.shape[0], fine_matrix.shape[1]
    half_x, half_y = count_x // 2, count_y // 2
    width, coarse_width = fine_matrix.shape[-1], box_ext.shape[-1]
    total = jnp.zeros((half_x, 2, half_y, 2, 2, 5, 5, width, coarse_width), jnp.float32)
    for direction in range(7):
        product = jnp.einsum('xyzpq,xyztqr->xyztpr', fine_matrix[:, :, :, direction].astype(jnp.float32),
                             views[direction].astype(jnp.float32))
        if direction > 0:
            product = product * face_links[:, :, :, direction - 1, None, None, None].astype(jnp.float32)
        product = product.reshape(half_x, 2, half_y, 2, 2, 3, 3, width, coarse_width)
        for parity_x in range(2):
            for parity_y in range(2):
                shift_x, shift_y = box_step(direction, parity_x, parity_y)
                total = total.at[:, parity_x, :, parity_y, :, 1 + shift_x:4 + shift_x, 1 + shift_y:4 + shift_y].add(
                    product[:, parity_x, :, parity_y])
    return total.astype(jnp.bfloat16).reshape(half_x, 2, half_y, 2, 2, 25, width, coarse_width)


def place_blocks(contrib):
    half_x, half_y = contrib.shape[0], contrib.shape[1]
    coarse_width = contrib.shape[-1]
    buffer = jnp.zeros((half_x + 2, half_y + 2, 7, 7, coarse_width, coarse_width), jnp.float32)
    for offset_x in range(3):
        for offset_y in range(3):
            piece = contrib[:, :, 3 * offset_x + offset_y].reshape(half_x, half_y, 5, 5, coarse_width, coarse_width)
            buffer = buffer.at[offset_x:offset_x + half_x, offset_y:offset_y + half_y,
                               2 - offset_x:7 - offset_x, 2 - offset_y:7 - offset_y].add(piece)
    return buffer


def reference(fine_matrix, prolongator, aggregate, face_links):
    boxes_y = NY // 2
    padded_agg = jnp.pad(aggregate, ((1, 1), (1, 1), (0, 0)))
    slot_table = slot_ids(padded_agg, face_links, jnp.int32(0), jnp.int32(0), boxes_y)

    def box_row(index):
        row_index = jnp.clip(index - 1, 0, NX - 1).astype(jnp.int32)
        valid = ((index >= 1) & (index <= NX)).astype(jnp.float32)
        blocks = lax.dynamic_index_in_dim(prolongator, row_index, 0, keepdims=False).astype(jnp.float32)
        table = lax.dynamic_index_in_dim(slot_table, row_index, 0, keepdims=False)
        selector = (table[..., None] == jnp.arange(9, dtype=jnp.int32)).astype(jnp.float32)
        return (jnp.einsum('yzmt,yzmpq->yztpq', selector, blocks) * valid).astype(jnp.bfloat16)

    box_rows = lax.map(box_row, jnp.arange(NX + 2, dtype=jnp.int32))

    def step_fn(window, index):
        start = (2 * index).astype(jnp.int32)
        matrix_rows = lax.dynamic_slice_in_dim(fine_matrix, start, 2, 0)
        link_rows = lax.dynamic_slice_in_dim(face_links, start, 2, 0)
        box_slab = lax.dynamic_slice_in_dim(box_rows, start, 4, 0)
        box_ext = jnp.pad(box_slab, ((0, 0), (1, 1), (0, 0), (0, 0), (0, 0), (0, 0)))
        image = image_blocks(matrix_rows, link_rows, box_ext)
        left = box_slab[1:3].reshape(1, 2, NY // 2, 2, 2, 9, B, CB)
        contrib = jnp.einsum('abcderkp,abcdeskq->acrspq', left.astype(jnp.float32), image.astype(jnp.float32))
        window = window + place_blocks(contrib)
        finished = window[0, 1:-1].astype(jnp.bfloat16)
        window = jnp.concatenate([window[1:], jnp.zeros_like(window[:1])], axis=0)
        return window, finished

    start_window = jnp.zeros((3, NY // 2 + 2, 7, 7, CB, CB), jnp.float32)
    window, finished = lax.scan(step_fn, start_window, jnp.arange(NX // 2, dtype=jnp.int32))
    last_row = window[0, 1:-1].astype(jnp.bfloat16)[None]
    return jnp.concatenate([finished[1:], last_row], axis=0)
```

```python
import functools

import jax
import jax.numpy as jnp
from jax import lax
from jax.experimental import pallas as pl
from jax.experimental.pallas import tpu as pltpu
from jax.sharding import PartitionSpec as P

MESH = pl.DeviceIdType.MESH
F32 = jnp.float32
BF16 = jnp.bfloat16

CORNERS = ((-1, -1), (-1, 1), (1, -1), (1, 1))
FACES = ((-1, 0), (1, 0), (0, -1), (0, 1))
NOWHERE = -1000000

EVENS = ((0, 0), (-1, 0), (1, 0), (-2, 0), (2, 0), (0, -2), (0, 2))
ODDS = ((0, -1), (0, 1), (-1, -1), (-1, 1), (1, -1), (1, 1), None)
PAIRS = tuple(zip(EVENS, ODDS))


def corner(sx, sy):
    return (2 if sx > 0 else 0) + (1 if sy > 0 else 0)


def element_tiles(sx, sy):
    return (((0, 0), (sx, sy)), ((sx, 0), (0, sy)), ((-sx, 0), (0, -sy)))


def image_tiles(sx, sy):
    return element_tiles(sx, sy) + (((2 * sx, 0), (sx, -sy)), ((0, 2 * sy), (-sx, sy)))


def slots(sx, sy):
    return (2 if sx < 0 else 1), (4 if sy < 0 else 3), (1 if sx < 0 else 2), (3 if sy < 0 else 4)


def add(u, v):
    return (u[0] + v[0], u[1] + v[1])


def dot(a, b):
    return jnp.dot(a, b, preferred_element_type=F32)


def kernel(
    nx, ny, a_hbm, p_hbm, agg, links, out,
    a_v, p_v, tab, gtab, part, tiles, gx, gy, mats, im, ptg, ptd, imw,
    face_out, face_in, diag_out, diag_in, acc,
    ld_sem, agg_s, agg_r, early_s, early_r, late_s, late_r, face_s, face_r, diag_s, diag_r,
):
    mx, my = lax.axis_index("sx"), lax.axis_index("sy")
    par = lax.rem(my, 2)

    def device(dx, dy):
        return (lax.rem(mx + dx + nx, nx), lax.rem(my + dy + ny, ny))

    def box_id(t):
        return (mx + t[0]) * ny + my + t[1]

    barrier = pltpu.get_barrier_semaphore()
    for d in FACES + CORNERS:
        pl.semaphore_signal(barrier, inc=1, device_id=device(*d), device_id_type=MESH)
    load_p = pltpu.make_async_copy(p_hbm, p_v, ld_sem.at[0])
    load_a = pltpu.make_async_copy(a_hbm, a_v, ld_sem.at[1])
    load_p.start()
    load_a.start()

    for x in range(2):
        for y in range(2):
            for z in range(2):
                tab[4 * x + 2 * y + z, :] = jnp.full((128,), agg[x, y, z], jnp.int32)

    half = (lax.broadcasted_iota(jnp.int32, (1, 128), 1) >= 64).astype(jnp.int32)
    even_row = half == par
    even = jnp.broadcast_to(((lax.broadcasted_iota(jnp.int32, (128, 128), 1) >= 64).astype(jnp.int32)) == par, (128, 128))

    def lane_ids(pair):
        return jnp.where(even_row, box_id(pair[0]), box_id(pair[1]))

    def doubled(x, y, z, m):
        block = p_v[x, y, z, m].astype(F32)
        return jnp.concatenate([block, block], axis=1)

    def picked(ids, target):
        return (ids == target).astype(F32)

    load_p.wait()
    for c, (sx, sy) in enumerate(CORNERS):
        x, y = (sx + 1) // 2, (sy + 1) // 2
        ix, iy, ox, oy = slots(sx, sy)
        ids = [lane_ids(pair) for pair in element_tiles(sx, sy)]
        for z in range(2):
            mz = 6 if z == 0 else 5
            total = [None, None, None]
            for m, (ex, ey, ez) in ((0, (x, y, z)), (mz, (x, y, 1 - z)), (ix, (1 - x, y, z)), (iy, (x, 1 - y, z))):
                target = agg[ex, ey, ez]
                if m > 0:
                    target = jnp.where(links[x, y, z, m - 1] == 1, target, NOWHERE)
                block = doubled(x, y, z, m)
                for t in range(3):
                    if t == 2 and m in (0, mz):
                        continue
                    term = block * picked(ids[t], target)
                    total[t] = term if total[t] is None else total[t] + term
            tiles[c, 2, 64 * z : 64 * z + 64, :] = total[2].astype(BF16)
            part[2 * c + z, 0] = total[0]
            part[2 * c + z, 1] = total[1]

    pl.semaphore_wait(barrier, 8)

    agg_copies = []
    for d, (dx, dy) in enumerate(FACES):
        agg_copies.append(
            pltpu.make_async_remote_copy(
                src_ref=tab, dst_ref=gtab.at[d], send_sem=agg_s.at[d], recv_sem=agg_r.at[d],
                device_id=device(-dx, -dy), device_id_type=MESH,
            )
        )
        agg_copies[-1].start()

    def ghost_copy(c, along_y, early):
        sx, sy = CORNERS[c]
        k = 4 + c if along_y else c
        src = tiles.at[corner(sx, -sy) if along_y else corner(-sx, sy)]
        dst = (gy if along_y else gx).at[c]
        part_of = pl.ds(2, 1) if early else pl.ds(0, 2)
        return pltpu.make_async_remote_copy(
            src_ref=src.at[part_of], dst_ref=dst.at[part_of],
            send_sem=(early_s if early else late_s).at[k], recv_sem=(early_r if early else late_r).at[k],
            device_id=device(0, -sy) if along_y else device(-sx, 0), device_id_type=MESH,
        )

    early_copies = {}
    for along_y in (True, False):
        for c in range(4):
            early_copies[along_y, c] = ghost_copy(c, along_y, True)
            early_copies[along_y, c].start()

    load_a.wait()
    for c, (sx, sy) in enumerate(CORNERS):
        x, y = (sx + 1) // 2, (sy + 1) // 2

        def block(z, m):
            value = a_v[x, y, z, m]
            if m == 0:
                return value
            return (value.astype(F32) * links[x, y, z, m - 1].astype(F32)).astype(BF16)

        mats[c, 0, 0:64, :] = jnp.concatenate([block(0, 0), block(0, 6)], axis=1)
        mats[c, 0, 64:128, :] = jnp.concatenate([block(1, 5), block(1, 0)], axis=1)
        zero = jnp.zeros((64, 64), BF16)
        for k, m in enumerate(slots(sx, sy)):
            mats[c, k + 1, 0:64, :] = jnp.concatenate([block(0, m), zero], axis=1)
            mats[c, k + 1, 64:128, :] = jnp.concatenate([zero, block(1, m)], axis=1)

    for copy in agg_copies:
        copy.wait_recv()
    late_copies = {}
    for c, (sx, sy) in enumerate(CORNERS):
        x, y = (sx + 1) // 2, (sy + 1) // 2
        ix, iy, ox, oy = slots(sx, sy)
        ids = [lane_ids(pair) for pair in element_tiles(sx, sy)]
        for z in range(2):
            row_x = gtab[FACES.index((sx, 0)), pl.ds(4 * (1 - x) + 2 * y + z, 1), :]
            row_y = gtab[FACES.index((0, sy)), pl.ds(4 * x + 2 * (1 - y) + z, 1), :]
            row_x = jnp.where(links[x, y, z, ox - 1] == 1, row_x, NOWHERE)
            row_y = jnp.where(links[x, y, z, oy - 1] == 1, row_y, NOWHERE)
            block_x, block_y = doubled(x, y, z, ox), doubled(x, y, z, oy)
            for t in range(2):
                total = part[2 * c + z, t] + block_x * picked(ids[t], row_x) + block_y * picked(ids[t], row_y)
                tiles[c, t, 64 * z : 64 * z + 64, :] = total.astype(BF16)
        for along_y, to in ((True, corner(sx, -sy)), (False, corner(-sx, sy))):
            late_copies[along_y, to] = ghost_copy(to, along_y, False)
            late_copies[along_y, to].start()

    top = jnp.full((64, 128), par, jnp.int32) == 0
    for c, (sx, sy) in enumerate(CORNERS):
        blocks = {}
        for t, pair in enumerate(element_tiles(sx, sy)):
            turned = tiles[c, t].astype(F32).T
            blocks[pair[0]] = jnp.where(top, turned[0:64], turned[64:128]).astype(BF16)
            blocks[pair[1]] = jnp.where(top, turned[64:128], turned[0:64]).astype(BF16)
        ptd[c] = blocks[sx, sy]
        for r, offset in enumerate(FACES + ((0, 0),)):
            ptg[64 * r : 64 * r + 64, 128 * c : 128 * c + 128] = blocks[offset]

    def product(mat, ref, c):
        rows = dot(mat, jnp.concatenate([ref[c, 0], ref[c, 1], ref[c, 2]], axis=1))
        return rows[:, 0:128], rows[:, 128:256], rows[:, 256:384]

    nothing = jnp.zeros((128, 128), F32)
    for c, (sx, sy) in enumerate(CORNERS):
        s0, s1, s2 = product(mats[c, 0], tiles, c)
        x0, x1, x2 = product(mats[c, 1], tiles, corner(-sx, sy))
        y0, y1, y2 = product(mats[c, 2], tiles, corner(sx, -sy))
        im[c, 0] = s0 + jnp.where(even, x0 + y0, nothing)
        im[c, 1] = s1 + jnp.where(even, x2 + y1, x1 + y2)
        im[c, 2] = s2 + jnp.where(even, x1 + y2, x2 + y1)
        im[c, 3] = jnp.where(even, nothing, y0)
        im[c, 4] = jnp.where(even, nothing, x0)

    for jx in range(7):
        for jy in range(7):
            if abs(jx - 3) + abs(jy - 3) > 3:
                out[0, 0, jx, jy] = jnp.zeros((64, 64), BF16)

    for copy in late_copies.values():
        pass
    diag_copies, face_copies = {}, {}
    for c, (sx, sy) in enumerate(CORNERS):
        early_copies[False, c].wait_recv()
        late_copies[False, c].wait_recv()
        early_copies[True, c].wait_recv()
        late_copies[True, c].wait_recv()
        x0, x1, x2 = product(mats[c, 3], gx, c)
        y0, y1, y2 = product(mats[c, 4], gy, c)
        image = [
            (im[c, 0] + x1 + y1).astype(BF16),
            (im[c, 1] + x0 + y0).astype(BF16),
            im[c, 2].astype(BF16),
            (im[c, 3] + x2).astype(BF16),
            (im[c, 4] + y2).astype(BF16),
        ]
        diag_out[c] = dot(ptd[c], jnp.concatenate(image, axis=1)).astype(BF16)
        to = corner(-sx, -sy)
        diag_copies[to] = pltpu.make_async_remote_copy(
            src_ref=diag_out.at[c], dst_ref=diag_in.at[to], send_sem=diag_s.at[to], recv_sem=diag_r.at[to],
            device_id=device(sx, sy), device_id_type=MESH,
        )
        diag_copies[to].start()
        names = image_tiles(sx, sy)
        at_even = {pair[0]: i for i, pair in enumerate(names)}
        at_odd = {pair[1]: i for i, pair in enumerate(names)}
        for g, (e, o) in enumerate(PAIRS):
            left = image[at_even[e]].astype(F32) if e in at_even else nothing
            right = image[at_odd[o]].astype(F32) if o in at_odd else nothing
            imw[128 * c : 128 * c + 128, 128 * g : 128 * g + 128] = jnp.where(even, left, right).astype(BF16)

    def send_face(d):
        dx, dy = FACES[d]
        to = FACES.index((-dx, -dy))
        face_copies[to] = pltpu.make_async_remote_copy(
            src_ref=face_out.at[d], dst_ref=face_in.at[to], send_sem=face_s.at[to], recv_sem=face_r.at[to],
            device_id=device(dx, dy), device_id_type=MESH,
        )
        face_copies[to].start()

    wide = imw[...]
    for first in (2, 0):
        rows = dot(ptg[64 * first : 64 * first + 128, :], wide).astype(BF16)
        for d in (first, first + 1):
            face_out[d] = rows[64 * (d - first) : 64 * (d - first) + 64]
            send_face(d)

    offsets = [(dx, dy) for dx in range(-3, 4) for dy in range(-3, 4) if abs(dx) + abs(dy) <= 3]
    at = {offset: i for i, offset in enumerate(offsets)}
    own = dot(ptg[256:320, :], wide)
    for offset in offsets:
        acc[at[offset]] = jnp.zeros((64, 128), F32)
    for g, pair in enumerate(PAIRS):
        for offset in pair:
            if offset is not None:
                acc[at[offset]] = own[:, 128 * g : 128 * g + 128]

    for d in (0, 1):
        face_copies[d].wait_recv()
        for g, pair in enumerate(PAIRS):
            tile = face_in[d, :, 128 * g : 128 * g + 128].astype(F32)
            for offset in pair:
                if offset is not None:
                    acc[at[add(offset, FACES[d])]] += tile
    for c, (sx, sy) in enumerate(CORNERS):
        diag_copies[c].wait_recv()
        for g, pair in enumerate(image_tiles(-sx, -sy)):
            tile = diag_in[c, :, 128 * g : 128 * g + 128].astype(F32)
            for offset in pair:
                acc[at[add(offset, (sx, sy))]] += tile
    for d in (2, 3):
        face_copies[d].wait_recv()
        for g, pair in enumerate(PAIRS):
            tile = face_in[d, :, 128 * g : 128 * g + 128].astype(F32)
            for offset in pair:
                if offset is not None:
                    acc[at[add(offset, FACES[d])]] += tile

    for offset in offsets:
        value = acc[at[offset]]
        other = pltpu.roll(value, 64, 1)
        first = top if offset[1] % 2 == 0 else jnp.logical_not(top)
        out[0, 0, offset[0] + 3, offset[1] + 3] = jnp.where(first, value, other)[:, 0:64].astype(BF16)

    for copies in (agg_copies, early_copies.values(), late_copies.values(), diag_copies.values(), face_copies.values()):
        for copy in copies:
            copy.wait_send()


def per_device(fine_matrix, prolongator, aggregate, face_links):
    nx, ny = lax.axis_size("sx"), lax.axis_size("sy")
    dma = pltpu.SemaphoreType.DMA
    return pl.pallas_call(
        functools.partial(kernel, nx, ny),
        out_shape=jax.ShapeDtypeStruct((1, 1, 7, 7, 64, 64), BF16),
        in_specs=[
            pl.BlockSpec(memory_space=pl.ANY),
            pl.BlockSpec(memory_space=pl.ANY),
            pl.BlockSpec(memory_space=pltpu.SMEM),
            pl.BlockSpec(memory_space=pltpu.SMEM),
        ],
        out_specs=pl.BlockSpec(memory_space=pltpu.VMEM),
        scratch_shapes=[
            pltpu.VMEM((2, 2, 2, 7, 64, 64), BF16),
            pltpu.VMEM((2, 2, 2, 7, 64, 64), BF16),
            pltpu.VMEM((8, 128), jnp.int32),
            pltpu.VMEM((4, 8, 128), jnp.int32),
            pltpu.VMEM((8, 2, 64, 128), F32),
            pltpu.VMEM((4, 3, 128, 128), BF16),
            pltpu.VMEM((4, 3, 128, 128), BF16),
            pltpu.VMEM((4, 3, 128, 128), BF16),
            pltpu.VMEM((4, 5, 128, 128), BF16),
            pltpu.VMEM((4, 5, 128, 128), F32),
            pltpu.VMEM((320, 512), BF16),
            pltpu.VMEM((4, 64, 128), BF16),
            pltpu.VMEM((512, 896), BF16),
            pltpu.VMEM((4, 64, 896), BF16),
            pltpu.VMEM((4, 64, 896), BF16),
            pltpu.VMEM((4, 64, 640), BF16),
            pltpu.VMEM((4, 64, 640), BF16),
            pltpu.VMEM((25, 64, 128), F32),
            dma((2,)),
            dma((4,)),
            dma((4,)),
            dma((8,)),
            dma((8,)),
            dma((8,)),
            dma((8,)),
            dma((4,)),
            dma((4,)),
            dma((4,)),
            dma((4,)),
        ],
        compiler_params=pltpu.CompilerParams(
            collective_id=0, has_side_effects=True, vmem_limit_bytes=32 * 1024 * 1024
        ),
        name="galerkin",
    )(fine_matrix, prolongator, aggregate, face_links)


def solution(mesh):
    return jax.shard_map(
        per_device,
        mesh=mesh,
        in_specs=(
            P("sx", "sy", None, None, None, None),
            P("sx", "sy", None, None, None, None),
            P("sx", "sy", None),
            P("sx", "sy", None, None),
        ),
        out_specs=P("sx", "sy", None, None, None, None),
        check_vma=False,
    )
```

```python
import functools

import jax
import jax.numpy as jnp
from jax import lax
from jax.experimental import pallas as pl
from jax.experimental.pallas import tpu as pltpu
from jax.sharding import PartitionSpec as P

MESH = pl.DeviceIdType.MESH
F32 = jnp.float32
BF16 = jnp.bfloat16

CORNERS = ((-1, -1), (-1, 1), (1, -1), (1, 1))
FACES = ((-1, 0), (1, 0), (0, -1), (0, 1))
DIRECTIONS = FACES + CORNERS
NOWHERE = -1000000
FACTS = 6

EVENS = ((0, 0), (-1, 0), (1, 0), (-2, 0), (2, 0), (0, -2), (0, 2))
ODDS = ((0, -1), (0, 1), (-1, -1), (-1, 1), (1, -1), (1, 1), None)
PAIRS = tuple(zip(EVENS, ODDS))


def corner(sx, sy):
    return (2 if sx > 0 else 0) + (1 if sy > 0 else 0)


def element_tiles(sx, sy):
    return (((0, 0), (sx, sy)), ((sx, 0), (0, sy)), ((-sx, 0), (0, -sy)))


def image_tiles(sx, sy):
    return element_tiles(sx, sy) + (((2 * sx, 0), (sx, -sy)), ((0, 2 * sy), (-sx, sy)))


def slots(sx, sy):
    return (2 if sx < 0 else 1), (4 if sy < 0 else 3), (1 if sx < 0 else 2), (3 if sy < 0 else 4)


def add(u, v):
    return (u[0] + v[0], u[1] + v[1])


def dot(a, b):
    return jnp.dot(a, b, preferred_element_type=F32)


def kernel(
    nx, ny, a_hbm, p_hbm, agg_hbm, links_hbm, out,
    a_v, p_v, agg, links, facts, facts_in, raw, raw_x, raw_y, tiles, tiles_x, tiles_y, mats, im, ptg, ptd, imw,
    face_out, face_in, first_out, first_in, rest_out, rest_in, acc,
    scalar_sem, p_sem, a_sem, facts_s, facts_r, raw_s, raw_r, face_s, face_r, first_s, first_r, rest_s, rest_r,
):
    mx, my = lax.axis_index("sx"), lax.axis_index("sy")
    par = lax.rem(my, 2)

    def device(dx, dy):
        return (lax.rem(mx + dx + nx, nx), lax.rem(my + dy + ny, ny))

    inside = {(-1, 0): mx > 0, (1, 0): mx < nx - 1, (0, -1): my > 0, (0, 1): my < ny - 1}
    for sx, sy in CORNERS:
        inside[sx, sy] = jnp.logical_and(inside[sx, 0], inside[0, sy])

    def when(d, action):
        pl.when(inside[d])(action)

    def remote(src, dst, sems, k, d):
        return pltpu.make_async_remote_copy(
            src_ref=src, dst_ref=dst, send_sem=sems[0].at[k], recv_sem=sems[1].at[k],
            device_id=device(*d), device_id_type=MESH,
        )

    barrier = pltpu.get_barrier_semaphore()
    for d in DIRECTIONS:
        when(d, lambda: pl.semaphore_signal(barrier, inc=1, device_id=device(*d), device_id_type=MESH))
    scalar_loads = (
        pltpu.make_async_copy(agg_hbm, agg, scalar_sem.at[0]),
        pltpu.make_async_copy(links_hbm, links, scalar_sem.at[1]),
    )
    p_loads, a_loads = [], []
    for c, (sx, sy) in enumerate(CORNERS):
        x, y = (sx + 1) // 2, (sy + 1) // 2
        p_loads.append(pltpu.make_async_copy(p_hbm.at[x, y], p_v.at[x, y], p_sem.at[c]))
        a_loads.append(pltpu.make_async_copy(a_hbm.at[x, y], a_v.at[x, y], a_sem.at[c]))
    for copy in (*scalar_loads, *p_loads, *a_loads):
        copy.start()

    left = lax.broadcasted_iota(jnp.int32, (1, 128), 1) < 64
    even_row = (lax.broadcasted_iota(jnp.int32, (1, 128), 1) >= 64).astype(jnp.int32) == par
    even = (lax.broadcasted_iota(jnp.int32, (128, 128), 1) >= 64).astype(jnp.int32) == par
    top = jnp.full((64, 128), par, jnp.int32) == 0

    for side in FACES:

        @pl.when(jnp.logical_not(inside[side]))
        def _():
            for c, (sx, sy) in enumerate(CORNERS):
                if side == (sx, 0):
                    raw_x[c] = jnp.zeros((3, 128, 128), BF16)
                if side == (0, sy):
                    raw_y[c] = jnp.zeros((3, 128, 128), BF16)

    def place(x, y, z, fact):
        return FACTS * (4 * x + 2 * y + z) + fact

    for copy in scalar_loads:
        copy.wait()
    for c, (sx, sy) in enumerate(CORNERS):
        x, y = (sx + 1) // 2, (sy + 1) // 2
        ix, iy, ox, oy = slots(sx, sy)
        for z in range(2):
            mz = 6 if z == 0 else 5
            mine = agg[x, y, z]
            facts[place(x, y, z, 0)] = mine
            for fact, m, target in (
                (1, mz, agg[x, y, 1 - z]), (2, ix, agg[1 - x, y, z]), (3, iy, agg[x, 1 - y, z]), (4, ox, mine), (5, oy, mine)
            ):
                facts[place(x, y, z, fact)] = jnp.where(links[x, y, z, m - 1] == 1, target, NOWHERE)

    for c, (sx, sy) in enumerate(CORNERS):
        x, y = (sx + 1) // 2, (sy + 1) // 2
        ix, iy, ox, oy = slots(sx, sy)
        p_loads[c].wait()
        for z in range(2):
            for j, (m, n) in enumerate(((0, 6 if z == 0 else 5), (ix, iy), (ox, oy))):
                raw[c, j, 64 * z : 64 * z + 64, :] = jnp.concatenate([p_v[x, y, z, m], p_v[x, y, z, n]], axis=1)

    pl.semaphore_wait(barrier, sum(there.astype(jnp.int32) for there in inside.values()))

    facts_copies = {}
    for k, (dx, dy) in enumerate(DIRECTIONS):
        facts_copies[dx, dy] = remote(facts, facts_in.at[k], (facts_s, facts_r), k, (-dx, -dy))
        when((-dx, -dy), facts_copies[dx, dy].start)
    copies_x, copies_y = [], []
    for c, (sx, sy) in enumerate(CORNERS):
        copies_x.append(remote(raw.at[corner(-sx, sy)], raw_x.at[c], (raw_s, raw_r), c, (-sx, 0)))
        copies_y.append(remote(raw.at[corner(sx, -sy)], raw_y.at[c], (raw_s, raw_r), 4 + c, (0, -sy)))
    for c, (sx, sy) in enumerate(CORNERS):
        when((0, -sy), copies_y[c].start)
    for c, (sx, sy) in enumerate(CORNERS):
        when((-sx, 0), copies_x[c].start)

    for c, (sx, sy) in enumerate(CORNERS):
        x, y = (sx + 1) // 2, (sy + 1) // 2
        a_loads[c].wait()

        def block(z, m):
            value = a_v[x, y, z, m]
            if m == 0:
                return value
            return (value.astype(F32) * links[x, y, z, m - 1].astype(F32)).astype(BF16)

        mats[c, 0, 0:64, :] = jnp.concatenate([block(0, 0), block(0, 6)], axis=1)
        mats[c, 0, 64:128, :] = jnp.concatenate([block(1, 5), block(1, 0)], axis=1)
        zero = jnp.zeros((64, 64), BF16)
        for k, m in enumerate(slots(sx, sy)):
            mats[c, k + 1, 0:64, :] = jnp.concatenate([block(0, m), zero], axis=1)
            mats[c, k + 1, 64:128, :] = jnp.concatenate([zero, block(1, m)], axis=1)

    def told(d, x, y, z, fact):
        return jnp.where(inside[d], facts_in[DIRECTIONS.index(d), place(x, y, z, fact)], NOWHERE)

    def combine(source, target, names, flipped, origin, targets):
        def lane_ids(pair):
            first, second = (((mx + origin[0] + t[0]) * ny + my + origin[1] + t[1]) for t in pair)
            return jnp.where(even_row, second, first) if flipped else jnp.where(even_row, first, second)

        ids = [lane_ids(pair) for pair in names]
        for z in range(2):
            rows = slice(64 * z, 64 * z + 64)
            boxes = targets(z)
            total = [None, None, None]
            for j in (1, 0, 2):
                straight = source[j, rows, :].astype(F32)
                turned = pltpu.roll(straight, 64, 1)
                for value, lanes in (
                    (straight, jnp.where(left, boxes[2 * j], boxes[2 * j + 1])),
                    (turned, jnp.where(left, boxes[2 * j + 1], boxes[2 * j])),
                ):
                    for t in range(3):
                        if t == 2 and j != 1:
                            continue
                        term = value * (lanes == ids[t]).astype(F32)
                        total[t] = term if total[t] is None else total[t] + term
            for t in range(3):
                target[t, rows, :] = total[t].astype(BF16)

    for d in DIRECTIONS:
        when(d, facts_copies[d].wait_recv)
    for c, (sx, sy) in enumerate(CORNERS):
        x, y = (sx + 1) // 2, (sy + 1) // 2
        combine(
            raw.at[c], tiles.at[c], element_tiles(sx, sy), False, (0, 0),
            lambda z: [facts[place(x, y, z, fact)] for fact in range(4)]
            + [told((sx, 0), 1 - x, y, z, 4), told((0, sy), x, 1 - y, z, 5)],
        )

    for c, (sx, sy) in enumerate(CORNERS):
        blocks = {}
        for t, pair in enumerate(element_tiles(sx, sy)):
            turned = tiles[c, t].astype(F32).T
            blocks[pair[0]] = jnp.where(top, turned[0:64], turned[64:128]).astype(BF16)
            blocks[pair[1]] = jnp.where(top, turned[64:128], turned[0:64]).astype(BF16)
        ptd[c] = blocks[sx, sy]
        for r, offset in enumerate(FACES + ((0, 0),)):
            ptg[64 * r : 64 * r + 64, 128 * c : 128 * c + 128] = blocks[offset]

    def product(mat, ref, c):
        rows = dot(mat, jnp.concatenate([ref[c, 0], ref[c, 1], ref[c, 2]], axis=1))
        return rows[:, 0:128], rows[:, 128:256], rows[:, 256:384]

    nothing = jnp.zeros((128, 128), F32)
    for c, (sx, sy) in enumerate(CORNERS):
        s0, s1, s2 = product(mats[c, 0], tiles, c)
        x0, x1, x2 = product(mats[c, 1], tiles, corner(-sx, sy))
        y0, y1, y2 = product(mats[c, 2], tiles, corner(sx, -sy))
        im[c, 0] = s0 + jnp.where(even, x0 + y0, nothing)
        im[c, 1] = s1 + jnp.where(even, x2 + y1, x1 + y2)
        im[c, 2] = s2 + jnp.where(even, x1 + y2, x2 + y1)
        im[c, 3] = jnp.where(even, nothing, y0)
        im[c, 4] = jnp.where(even, nothing, x0)

    for jx in range(7):
        for jy in range(7):
            if abs(jx - 3) + abs(jy - 3) > 3:
                out[0, 0, jx, jy] = jnp.zeros((64, 64), BF16)

    first_copies, rest_copies, face_copies = {}, {}, {}
    for c, (sx, sy) in enumerate(CORNERS):
        x, y = (sx + 1) // 2, (sy + 1) // 2
        when((sx, 0), copies_x[c].wait_recv)
        combine(
            raw_x.at[c], tiles_x.at[c], element_tiles(-sx, sy), False, (sx, 0),
            lambda z: [told((sx, 0), 1 - x, y, z, fact) for fact in range(4)]
            + [facts[place(x, y, z, 4)], told((sx, sy), 1 - x, 1 - y, z, 5)],
        )
        x0, x1, x2 = product(mats[c, 3], tiles_x, c)
        im[c, 0] += x1
        im[c, 1] += x0
        im[c, 3] += x2
        first = jnp.concatenate([im[c, 2].astype(BF16), im[c, 3].astype(BF16)], axis=1)
        first_out[c] = dot(ptd[c], first).astype(BF16)
        to = corner(-sx, -sy)
        first_copies[to] = remote(first_out.at[c], first_in.at[to], (first_s, first_r), to, (sx, sy))
        when((sx, sy), first_copies[to].start)

    for c, (sx, sy) in enumerate(CORNERS):
        x, y = (sx + 1) // 2, (sy + 1) // 2
        when((0, sy), copies_y[c].wait_recv)
        combine(
            raw_y.at[c], tiles_y.at[c], element_tiles(sx, -sy), True, (0, sy),
            lambda z: [told((0, sy), x, 1 - y, z, fact) for fact in range(4)]
            + [told((sx, sy), 1 - x, 1 - y, z, 4), facts[place(x, y, z, 5)]],
        )
        y0, y1, y2 = product(mats[c, 4], tiles_y, c)
        image = [
            (im[c, 0] + y1).astype(BF16), (im[c, 1] + y0).astype(BF16), im[c, 2].astype(BF16),
            im[c, 3].astype(BF16), (im[c, 4] + y2).astype(BF16),
        ]
        rest_out[c] = dot(ptd[c], jnp.concatenate([image[0], image[1], image[4]], axis=1)).astype(BF16)
        to = corner(-sx, -sy)
        rest_copies[to] = remote(rest_out.at[c], rest_in.at[to], (rest_s, rest_r), to, (sx, sy))
        when((sx, sy), rest_copies[to].start)
        names = image_tiles(sx, sy)
        at_even = {pair[0]: i for i, pair in enumerate(names)}
        at_odd = {pair[1]: i for i, pair in enumerate(names)}
        for g, (e, o) in enumerate(PAIRS):
            evens = image[at_even[e]].astype(F32) if e in at_even else nothing
            odds = image[at_odd[o]].astype(F32) if o in at_odd else nothing
            imw[128 * c : 128 * c + 128, 128 * g : 128 * g + 128] = jnp.where(even, evens, odds).astype(BF16)

    wide = imw[...]
    for first in (2, 0):
        rows = dot(ptg[64 * first : 64 * first + 128, :], wide).astype(BF16)
        for k in (first, first + 1):
            dx, dy = FACES[k]
            to = FACES.index((-dx, -dy))
            face_out[k] = rows[64 * (k - first) : 64 * (k - first) + 64]
            face_copies[to] = remote(face_out.at[k], face_in.at[to], (face_s, face_r), to, (dx, dy))
            when((dx, dy), face_copies[to].start)

    offsets = [(dx, dy) for dx in range(-3, 4) for dy in range(-3, 4) if abs(dx) + abs(dy) <= 3]
    at = {offset: i for i, offset in enumerate(offsets)}
    own = dot(ptg[256:320, :], wide)
    for offset in offsets:
        acc[at[offset]] = jnp.zeros((64, 128), F32)
    for g, pair in enumerate(PAIRS):
        for offset in pair:
            if offset is not None:
                acc[at[offset]] = own[:, 128 * g : 128 * g + 128]

    def gather(d, copy, ref, names):
        def action():
            copy.wait_recv()
            for g, pair in enumerate(names):
                tile = ref[:, 128 * g : 128 * g + 128].astype(F32)
                for offset in pair:
                    if offset is not None:
                        acc[at[add(offset, d)]] += tile

        when(d, action)

    for c, (sx, sy) in enumerate(CORNERS):
        gather((sx, sy), first_copies[c], first_in.at[c], image_tiles(-sx, -sy)[2:4])
    for k in (0, 1):
        gather(FACES[k], face_copies[k], face_in.at[k], PAIRS)
    for c, (sx, sy) in enumerate(CORNERS):
        names = image_tiles(-sx, -sy)
        gather((sx, sy), rest_copies[c], rest_in.at[c], (names[0], names[1], names[4]))
    for k in (2, 3):
        gather(FACES[k], face_copies[k], face_in.at[k], PAIRS)

    for offset in offsets:
        value = acc[at[offset]]
        other = pltpu.roll(value, 64, 1)
        straight = top if offset[1] % 2 == 0 else jnp.logical_not(top)
        out[0, 0, offset[0] + 3, offset[1] + 3] = jnp.where(straight, value, other)[:, 0:64].astype(BF16)

    for dx, dy in DIRECTIONS:
        when((-dx, -dy), facts_copies[dx, dy].wait_send)
    for k, (dx, dy) in enumerate(FACES):
        when((-dx, -dy), face_copies[k].wait_send)
    for c, (sx, sy) in enumerate(CORNERS):
        when((-sx, 0), copies_x[c].wait_send)
        when((0, -sy), copies_y[c].wait_send)
        when((-sx, -sy), first_copies[c].wait_send)
        when((-sx, -sy), rest_copies[c].wait_send)


def per_device(fine_matrix, prolongator, aggregate, face_links):
    nx, ny = lax.axis_size("sx"), lax.axis_size("sy")
    dma = pltpu.SemaphoreType.DMA
    return pl.pallas_call(
        functools.partial(kernel, nx, ny),
        out_shape=jax.ShapeDtypeStruct((1, 1, 7, 7, 64, 64), BF16),
        in_specs=[pl.BlockSpec(memory_space=pl.ANY)] * 4,
        out_specs=pl.BlockSpec(memory_space=pltpu.VMEM),
        scratch_shapes=[
            pltpu.VMEM((2, 2, 2, 7, 64, 64), BF16),
            pltpu.VMEM((2, 2, 2, 7, 64, 64), BF16),
            pltpu.SMEM((2, 2, 2), jnp.int32),
            pltpu.SMEM((2, 2, 2, 6), jnp.int32),
            pltpu.SMEM((64,), jnp.int32),
            pltpu.SMEM((8, 64), jnp.int32),
            *[pltpu.VMEM((4, 3, 128, 128), BF16)] * 6,
            pltpu.VMEM((4, 5, 128, 128), BF16),
            pltpu.VMEM((4, 5, 128, 128), F32),
            pltpu.VMEM((320, 512), BF16),
            pltpu.VMEM((4, 64, 128), BF16),
            pltpu.VMEM((512, 896), BF16),
            *[pltpu.VMEM((4, 64, 896), BF16)] * 2,
            *[pltpu.VMEM((4, 64, 256), BF16)] * 2,
            *[pltpu.VMEM((4, 64, 384), BF16)] * 2,
            pltpu.VMEM((25, 64, 128), F32),
            dma((2,)),
            dma((4,)),
            dma((4,)),
            *[dma((8,))] * 4,
            *[dma((4,))] * 6,
        ],
        compiler_params=pltpu.CompilerParams(
            collective_id=0, has_side_effects=True, vmem_limit_bytes=60 * 1024 * 1024
        ),
        name="galerkin",
    )(fine_matrix, prolongator, aggregate, face_links)


def solution(mesh):
    return jax.shard_map(
        per_device,
        mesh=mesh,
        in_specs=(
            P("sx", "sy", None, None, None, None),
            P("sx", "sy", None, None, None, None),
            P("sx", "sy", None),
            P("sx", "sy", None, None),
        ),
        out_specs=P("sx", "sy", None, None, None, None),
        check_vma=False,
    )
```

```python
import functools

import jax
import jax.numpy as jnp
from jax import lax
from jax.experimental import pallas as pl
from jax.experimental.pallas import tpu as pltpu
from jax.sharding import PartitionSpec as P

MESH = pl.DeviceIdType.MESH
F32 = jnp.float32
BF16 = jnp.bfloat16

CORNERS = ((-1, -1), (-1, 1), (1, -1), (1, 1))
FACES = ((-1, 0), (1, 0), (0, -1), (0, 1))
DIRECTIONS = FACES + CORNERS
NOWHERE = -1000000
FACTS = 6

EVENS = ((0, 0), (-1, 0), (1, 0), (-2, 0), (2, 0), (0, -2), (0, 2))
ODDS = ((0, -1), (0, 1), (-1, -1), (-1, 1), (1, -1), (1, 1), None)
PAIRS = tuple(zip(EVENS, ODDS))


def corner(sx, sy):
    return (2 if sx > 0 else 0) + (1 if sy > 0 else 0)


def element_tiles(sx, sy):
    return (((0, 0), (sx, sy)), ((sx, 0), (0, sy)), ((-sx, 0), (0, -sy)))


def image_tiles(sx, sy):
    return element_tiles(sx, sy) + (((2 * sx, 0), (sx, -sy)), ((0, 2 * sy), (-sx, sy)))


def slots(sx, sy):
    return (2 if sx < 0 else 1), (4 if sy < 0 else 3), (1 if sx < 0 else 2), (3 if sy < 0 else 4)


def add(u, v):
    return (u[0] + v[0], u[1] + v[1])


def dot(a, b):
    return jnp.dot(a, b, preferred_element_type=F32)


def kernel(
    nx, ny, a_hbm, p_hbm, agg_hbm, links_hbm, out,
    a_v, p_v, agg, links, facts, facts_in, raw, raw_x, raw_y, tiles, tiles_x, tiles_y, mats, im, ptg, ptd, imw,
    face_out, face_in, first_out, first_in, rest_out, rest_in, acc,
    scalar_sem, p_sem, a_sem, facts_s, facts_r, raw_s, raw_r, face_s, face_r, first_s, first_r, rest_s, rest_r,
):
    mx, my = lax.axis_index("sx"), lax.axis_index("sy")
    par = lax.rem(my, 2)

    def device(dx, dy):
        return (lax.rem(mx + dx + nx, nx), lax.rem(my + dy + ny, ny))

    inside = {(-1, 0): mx > 0, (1, 0): mx < nx - 1, (0, -1): my > 0, (0, 1): my < ny - 1}
    for sx, sy in CORNERS:
        inside[sx, sy] = jnp.logical_and(inside[sx, 0], inside[0, sy])

    def when(d, action):
        pl.when(inside[d])(action)

    def remote(src, dst, sems, k, d):
        return pltpu.make_async_remote_copy(
            src_ref=src, dst_ref=dst, send_sem=sems[0].at[k], recv_sem=sems[1].at[k],
            device_id=device(*d), device_id_type=MESH,
        )

    barrier = pltpu.get_barrier_semaphore()
    for d in DIRECTIONS:
        when(d, lambda: pl.semaphore_signal(barrier, inc=1, device_id=device(*d), device_id_type=MESH))
    scalar_loads = (
        pltpu.make_async_copy(agg_hbm, agg, scalar_sem.at[0]),
        pltpu.make_async_copy(links_hbm, links, scalar_sem.at[1]),
    )
    p_loads, a_loads = [], []
    for c, (sx, sy) in enumerate(CORNERS):
        x, y = (sx + 1) // 2, (sy + 1) // 2
        p_loads.append(pltpu.make_async_copy(p_hbm.at[x, y], p_v.at[x, y], p_sem.at[c]))
        a_loads.append(pltpu.make_async_copy(a_hbm.at[x, y], a_v.at[x, y], a_sem.at[c]))
    for copy in (*scalar_loads, *p_loads, *a_loads):
        copy.start()

    left = lax.broadcasted_iota(jnp.int32, (1, 128), 1) < 64
    even_row = (lax.broadcasted_iota(jnp.int32, (1, 128), 1) >= 64).astype(jnp.int32) == par
    even = (lax.broadcasted_iota(jnp.int32, (128, 128), 1) >= 64).astype(jnp.int32) == par
    top = jnp.full((64, 128), par, jnp.int32) == 0

    for side in FACES:

        @pl.when(jnp.logical_not(inside[side]))
        def _():
            for c, (sx, sy) in enumerate(CORNERS):
                if side == (sx, 0):
                    raw_x[c] = jnp.zeros((3, 128, 128), BF16)
                if side == (0, sy):
                    raw_y[c] = jnp.zeros((3, 128, 128), BF16)

    def place(x, y, z, fact):
        return FACTS * (4 * x + 2 * y + z) + fact

    for copy in scalar_loads:
        copy.wait()
    for c, (sx, sy) in enumerate(CORNERS):
        x, y = (sx + 1) // 2, (sy + 1) // 2
        ix, iy, ox, oy = slots(sx, sy)
        for z in range(2):
            mz = 6 if z == 0 else 5
            mine = agg[x, y, z]
            facts[place(x, y, z, 0)] = mine
            for fact, m, target in (
                (1, mz, agg[x, y, 1 - z]), (2, ix, agg[1 - x, y, z]), (3, iy, agg[x, 1 - y, z]), (4, ox, mine), (5, oy, mine)
            ):
                facts[place(x, y, z, fact)] = jnp.where(links[x, y, z, m - 1] == 1, target, NOWHERE)

    for c, (sx, sy) in enumerate(CORNERS):
        x, y = (sx + 1) // 2, (sy + 1) // 2
        ix, iy, ox, oy = slots(sx, sy)
        p_loads[c].wait()
        for z in range(2):
            for j, (m, n) in enumerate(((0, 6 if z == 0 else 5), (ix, iy), (ox, oy))):
                raw[c, j, 64 * z : 64 * z + 64, :] = jnp.concatenate([p_v[x, y, z, m], p_v[x, y, z, n]], axis=1)

    pl.semaphore_wait(barrier, sum(there.astype(jnp.int32) for there in inside.values()))

    facts_copies = {}
    for k, (dx, dy) in enumerate(DIRECTIONS):
        facts_copies[dx, dy] = remote(facts, facts_in.at[k], (facts_s, facts_r), k, (-dx, -dy))
        when((-dx, -dy), facts_copies[dx, dy].start)
    copies_x, copies_y = [], []
    for c, (sx, sy) in enumerate(CORNERS):
        copies_x.append(remote(raw.at[corner(-sx, sy)], raw_x.at[c], (raw_s, raw_r), c, (-sx, 0)))
        copies_y.append(remote(raw.at[corner(sx, -sy)], raw_y.at[c], (raw_s, raw_r), 4 + c, (0, -sy)))
    for c, (sx, sy) in enumerate(CORNERS):
        when((0, -sy), copies_y[c].start)
    for c, (sx, sy) in enumerate(CORNERS):
        when((-sx, 0), copies_x[c].start)

    for c, (sx, sy) in enumerate(CORNERS):
        x, y = (sx + 1) // 2, (sy + 1) // 2
        a_loads[c].wait()

        def block(z, m):
            value = a_v[x, y, z, m]
            if m == 0:
                return value
            return (value.astype(F32) * links[x, y, z, m - 1].astype(F32)).astype(BF16)

        mats[c, 0, 0:64, :] = jnp.concatenate([block(0, 0), block(0, 6)], axis=1)
        mats[c, 0, 64:128, :] = jnp.concatenate([block(1, 5), block(1, 0)], axis=1)
        zero = jnp.zeros((64, 64), BF16)
        for k, m in enumerate(slots(sx, sy)):
            mats[c, k + 1, 0:64, :] = jnp.concatenate([block(0, m), zero], axis=1)
            mats[c, k + 1, 64:128, :] = jnp.concatenate([zero, block(1, m)], axis=1)

    def told(d, x, y, z, fact):
        return jnp.where(inside[d], facts_in[DIRECTIONS.index(d), place(x, y, z, fact)], NOWHERE)

    def combine(source, target, names, flipped, origin, targets):
        def lane_ids(pair):
            first, second = (((mx + origin[0] + t[0]) * ny + my + origin[1] + t[1]) for t in pair)
            return jnp.where(even_row, second, first) if flipped else jnp.where(even_row, first, second)

        ids = [lane_ids(pair) for pair in names]
        for z in range(2):
            rows = slice(64 * z, 64 * z + 64)
            boxes = targets(z)
            total = [None, None, None]
            for j in (1, 0, 2):
                straight = source[j, rows, :].astype(F32)
                turned = pltpu.roll(straight, 64, 1)
                for value, lanes in (
                    (straight, jnp.where(left, boxes[2 * j], boxes[2 * j + 1])),
                    (turned, jnp.where(left, boxes[2 * j + 1], boxes[2 * j])),
                ):
                    for t in range(3):
                        if t == 2 and j != 1:
                            continue
                        term = value * (lanes == ids[t]).astype(F32)
                        total[t] = term if total[t] is None else total[t] + term
            for t in range(3):
                target[t, rows, :] = total[t].astype(BF16)

    for d in DIRECTIONS:
        when(d, facts_copies[d].wait_recv)
    for c, (sx, sy) in enumerate(CORNERS):
        x, y = (sx + 1) // 2, (sy + 1) // 2
        combine(
            raw.at[c], tiles.at[c], element_tiles(sx, sy), False, (0, 0),
            lambda z: [facts[place(x, y, z, fact)] for fact in range(4)]
            + [told((sx, 0), 1 - x, y, z, 4), told((0, sy), x, 1 - y, z, 5)],
        )

    for c, (sx, sy) in enumerate(CORNERS):
        blocks = {}
        for t, pair in enumerate(element_tiles(sx, sy)):
            turned = tiles[c, t].astype(F32).T
            blocks[pair[0]] = jnp.where(top, turned[0:64], turned[64:128]).astype(BF16)
            blocks[pair[1]] = jnp.where(top, turned[64:128], turned[0:64]).astype(BF16)
        ptd[c] = blocks[sx, sy]
        for r, offset in enumerate(FACES + ((0, 0),)):
            ptg[64 * r : 64 * r + 64, 128 * c : 128 * c + 128] = blocks[offset]

    def product(mat, ref, c):
        rows = dot(mat, jnp.concatenate([ref[c, 0], ref[c, 1], ref[c, 2]], axis=1))
        return rows[:, 0:128], rows[:, 128:256], rows[:, 256:384]

    nothing = jnp.zeros((128, 128), F32)
    for c, (sx, sy) in enumerate(CORNERS):
        s0, s1, s2 = product(mats[c, 0], tiles, c)
        x0, x1, x2 = product(mats[c, 1], tiles, corner(-sx, sy))
        y0, y1, y2 = product(mats[c, 2], tiles, corner(sx, -sy))
        im[c, 0] = s0 + jnp.where(even, x0 + y0, nothing)
        im[c, 1] = s1 + jnp.where(even, x2 + y1, x1 + y2)
        im[c, 2] = s2 + jnp.where(even, x1 + y2, x2 + y1)
        im[c, 3] = jnp.where(even, nothing, y0)
        im[c, 4] = jnp.where(even, nothing, x0)

    for jx in range(7):
        for jy in range(7):
            if abs(jx - 3) + abs(jy - 3) > 3:
                out[0, 0, jx, jy] = jnp.zeros((64, 64), BF16)

    first_copies, rest_copies, face_copies = {}, {}, {}
    for c, (sx, sy) in enumerate(CORNERS):
        x, y = (sx + 1) // 2, (sy + 1) // 2
        when((sx, 0), copies_x[c].wait_recv)
        combine(
            raw_x.at[c], tiles_x.at[c], element_tiles(-sx, sy), False, (sx, 0),
            lambda z: [told((sx, 0), 1 - x, y, z, fact) for fact in range(4)]
            + [facts[place(x, y, z, 4)], told((sx, sy), 1 - x, 1 - y, z, 5)],
        )
        x0, x1, x2 = product(mats[c, 3], tiles_x, c)
        im[c, 0] += x1
        im[c, 1] += x0
        im[c, 3] += x2
        first = jnp.concatenate([im[c, 2].astype(BF16), im[c, 3].astype(BF16)], axis=1)
        first_out[c] = dot(ptd[c], first).astype(BF16)
        to = corner(-sx, -sy)
        first_copies[to] = remote(first_out.at[c], first_in.at[to], (first_s, first_r), to, (sx, sy))
        when((sx, sy), first_copies[to].start)

    for c, (sx, sy) in enumerate(CORNERS):
        x, y = (sx + 1) // 2, (sy + 1) // 2
        when((0, sy), copies_y[c].wait_recv)
        combine(
            raw_y.at[c], tiles_y.at[c], element_tiles(sx, -sy), True, (0, sy),
            lambda z: [told((0, sy), x, 1 - y, z, fact) for fact in range(4)]
            + [told((sx, sy), 1 - x, 1 - y, z, 4), facts[place(x, y, z, 5)]],
        )
        y0, y1, y2 = product(mats[c, 4], tiles_y, c)
        image = [
            (im[c, 0] + y1).astype(BF16), (im[c, 1] + y0).astype(BF16), im[c, 2].astype(BF16),
            im[c, 3].astype(BF16), (im[c, 4] + y2).astype(BF16),
        ]
        rest_out[c] = dot(ptd[c], jnp.concatenate([image[0], image[1], image[4]], axis=1)).astype(BF16)
        to = corner(-sx, -sy)
        rest_copies[to] = remote(rest_out.at[c], rest_in.at[to], (rest_s, rest_r), to, (sx, sy))
        when((sx, sy), rest_copies[to].start)
        names = image_tiles(sx, sy)
        at_even = {pair[0]: i for i, pair in enumerate(names)}
        at_odd = {pair[1]: i for i, pair in enumerate(names)}
        for g, (e, o) in enumerate(PAIRS):
            evens = image[at_even[e]].astype(F32) if e in at_even else nothing
            odds = image[at_odd[o]].astype(F32) if o in at_odd else nothing
            imw[128 * c : 128 * c + 128, 128 * g : 128 * g + 128] = jnp.where(even, evens, odds).astype(BF16)

    wide = imw[...]
    for first in (2, 0):
        rows = dot(ptg[64 * first : 64 * first + 128, :], wide).astype(BF16)
        for k in (first, first + 1):
            dx, dy = FACES[k]
            to = FACES.index((-dx, -dy))
            face_out[k] = rows[64 * (k - first) : 64 * (k - first) + 64]
            face_copies[to] = remote(face_out.at[k], face_in.at[to], (face_s, face_r), to, (dx, dy))
            when((dx, dy), face_copies[to].start)

    offsets = [(dx, dy) for dx in range(-3, 4) for dy in range(-3, 4) if abs(dx) + abs(dy) <= 3]
    at = {offset: i for i, offset in enumerate(offsets)}
    own = dot(ptg[256:320, :], wide)
    for offset in offsets:
        acc[at[offset]] = jnp.zeros((64, 128), F32)
    for g, pair in enumerate(PAIRS):
        for offset in pair:
            if offset is not None:
                acc[at[offset]] = own[:, 128 * g : 128 * g + 128]

    def gather(d, copy, ref, names):
        def action():
            copy.wait_recv()
            for g, pair in enumerate(names):
                tile = ref[:, 128 * g : 128 * g + 128].astype(F32)
                for offset in pair:
                    if offset is not None:
                        acc[at[add(offset, d)]] += tile

        when(d, action)

    for c, (sx, sy) in enumerate(CORNERS):
        gather((sx, sy), first_copies[c], first_in.at[c], image_tiles(-sx, -sy)[2:4])
    for k in (0, 1):
        gather(FACES[k], face_copies[k], face_in.at[k], PAIRS)
    for c, (sx, sy) in enumerate(CORNERS):
        names = image_tiles(-sx, -sy)
        gather((sx, sy), rest_copies[c], rest_in.at[c], (names[0], names[1], names[4]))
    for k in (2, 3):
        gather(FACES[k], face_copies[k], face_in.at[k], PAIRS)

    for offset in offsets:
        value = acc[at[offset]]
        other = pltpu.roll(value, 64, 1)
        straight = top if offset[1] % 2 == 0 else jnp.logical_not(top)
        out[0, 0, offset[0] + 3, offset[1] + 3] = jnp.where(straight, value, other)[:, 0:64].astype(BF16)

    for dx, dy in DIRECTIONS:
        when((-dx, -dy), facts_copies[dx, dy].wait_send)
    for k, (dx, dy) in enumerate(FACES):
        when((-dx, -dy), face_copies[k].wait_send)
    for c, (sx, sy) in enumerate(CORNERS):
        when((-sx, 0), copies_x[c].wait_send)
        when((0, -sy), copies_y[c].wait_send)
        when((-sx, -sy), first_copies[c].wait_send)
        when((-sx, -sy), rest_copies[c].wait_send)


def per_device(fine_matrix, prolongator, aggregate, face_links):
    nx, ny = lax.axis_size("sx"), lax.axis_size("sy")
    dma = pltpu.SemaphoreType.DMA
    return pl.pallas_call(
        functools.partial(kernel, nx, ny),
        out_shape=jax.ShapeDtypeStruct((1, 1, 7, 7, 64, 64), BF16),
        in_specs=[pl.BlockSpec(memory_space=pl.ANY)] * 4,
        out_specs=pl.BlockSpec(memory_space=pltpu.VMEM),
        scratch_shapes=[
            pltpu.VMEM((2, 2, 2, 7, 64, 64), BF16),
            pltpu.VMEM((2, 2, 2, 7, 64, 64), BF16),
            pltpu.SMEM((2, 2, 2), jnp.int32),
            pltpu.SMEM((2, 2, 2, 6), jnp.int32),
            pltpu.SMEM((64,), jnp.int32),
            pltpu.SMEM((8, 64), jnp.int32),
            *[pltpu.VMEM((4, 3, 128, 128), BF16)] * 6,
            pltpu.VMEM((4, 5, 128, 128), BF16),
            pltpu.VMEM((4, 5, 128, 128), F32),
            pltpu.VMEM((320, 512), BF16),
            pltpu.VMEM((4, 64, 128), BF16),
            pltpu.VMEM((512, 896), BF16),
            *[pltpu.VMEM((4, 64, 896), BF16)] * 2,
            *[pltpu.VMEM((4, 64, 256), BF16)] * 2,
            *[pltpu.VMEM((4, 64, 384), BF16)] * 2,
            pltpu.VMEM((25, 64, 128), F32),
            dma((2,)),
            dma((4,)),
            dma((4,)),
            *[dma((8,))] * 4,
            *[dma((4,))] * 6,
        ],
        compiler_params=pltpu.CompilerParams(
            collective_id=0, has_side_effects=True, vmem_limit_bytes=32 * 1024 * 1024
        ),
        name="galerkin",
    )(*(pltpu.with_memory_space_constraint(v, pltpu.HBM) for v in (fine_matrix, prolongator, aggregate, face_links)))


def solution(mesh):
    return jax.shard_map(
        per_device,
        mesh=mesh,
        in_specs=(
            P("sx", "sy", None, None, None, None),
            P("sx", "sy", None, None, None, None),
            P("sx", "sy", None),
            P("sx", "sy", None, None),
        ),
        out_specs=P("sx", "sy", None, None, None, None),
        check_vma=False,
    )
```

```python
import functools

import jax
import jax.numpy as jnp
from jax import lax
from jax.experimental import pallas as pl
from jax.experimental.pallas import tpu as pltpu
from jax.sharding import PartitionSpec as P

MESH = pl.DeviceIdType.MESH
F32 = jnp.float32
BF16 = jnp.bfloat16

CORNERS = ((-1, -1), (-1, 1), (1, -1), (1, 1))
FACES = ((-1, 0), (1, 0), (0, -1), (0, 1))
DIRECTIONS = FACES + CORNERS
NOWHERE = -1000000
FACTS = 6

EVENS = ((0, 0), (-1, 0), (1, 0), (-2, 0), (2, 0), (0, -2), (0, 2))
ODDS = ((0, -1), (0, 1), (-1, -1), (-1, 1), (1, -1), (1, 1), None)
PAIRS = tuple(zip(EVENS, ODDS))


def corner(sx, sy):
    return (2 if sx > 0 else 0) + (1 if sy > 0 else 0)


def element_tiles(sx, sy):
    return (((0, 0), (sx, sy)), ((sx, 0), (0, sy)), ((-sx, 0), (0, -sy)))


def image_tiles(sx, sy):
    return element_tiles(sx, sy) + (((2 * sx, 0), (sx, -sy)), ((0, 2 * sy), (-sx, sy)))


def slots(sx, sy):
    return (2 if sx < 0 else 1), (4 if sy < 0 else 3), (1 if sx < 0 else 2), (3 if sy < 0 else 4)


def add(u, v):
    return (u[0] + v[0], u[1] + v[1])


def dot(a, b):
    return jnp.dot(a, b, preferred_element_type=F32)


def kernel(
    nx, ny, a_hbm, p_hbm, agg_hbm, links_hbm, out,
    a_v, p_v, agg, links, facts, facts_in, raw, raw_x, raw_y, tiles, tiles_x, tiles_y, mats, im, ptg, ptd, imw,
    face_out, face_in, first_out, first_in, rest_out, rest_in, acc,
    scalar_sem, p_sem, a_sem, facts_s, facts_r, raw_s, raw_r, face_s, face_r, first_s, first_r, rest_s, rest_r,
):
    mx, my = lax.axis_index("sx"), lax.axis_index("sy")
    par = lax.rem(my, 2)

    def device(dx, dy):
        return (lax.rem(mx + dx + nx, nx), lax.rem(my + dy + ny, ny))

    inside = {(-1, 0): mx > 0, (1, 0): mx < nx - 1, (0, -1): my > 0, (0, 1): my < ny - 1}
    for sx, sy in CORNERS:
        inside[sx, sy] = jnp.logical_and(inside[sx, 0], inside[0, sy])

    interior = jnp.logical_and(
        jnp.logical_and(inside[-1, 0], inside[1, 0]), jnp.logical_and(inside[0, -1], inside[0, 1])
    )

    def each(actions):
        @pl.when(interior)
        def _():
            for _, action in actions:
                action()

        @pl.when(jnp.logical_not(interior))
        def _():
            for d, action in actions:
                pl.when(inside[d])(action)

    def remote(src, dst, sems, k, d):
        return pltpu.make_async_remote_copy(
            src_ref=src, dst_ref=dst, send_sem=sems[0].at[k], recv_sem=sems[1].at[k],
            device_id=device(*d), device_id_type=MESH,
        )

    barrier = pltpu.get_barrier_semaphore()
    def greet(d):
        return d, lambda: pl.semaphore_signal(barrier, inc=1, device_id=device(*d), device_id_type=MESH)

    each([greet(d) for d in DIRECTIONS])
    scalar_loads = (
        pltpu.make_async_copy(agg_hbm, agg, scalar_sem.at[0]),
        pltpu.make_async_copy(links_hbm, links, scalar_sem.at[1]),
    )
    p_loads, a_loads = [], []
    for c, (sx, sy) in enumerate(CORNERS):
        x, y = (sx + 1) // 2, (sy + 1) // 2
        p_loads.append(pltpu.make_async_copy(p_hbm.at[x, y], p_v.at[x, y], p_sem.at[c]))
        a_loads.append(pltpu.make_async_copy(a_hbm.at[x, y], a_v.at[x, y], a_sem.at[c]))
    for copy in (*scalar_loads, *p_loads, *a_loads):
        copy.start()

    even_row = (lax.broadcasted_iota(jnp.int32, (1, 128), 1) >= 64).astype(jnp.int32) == par
    even = (lax.broadcasted_iota(jnp.int32, (128, 128), 1) >= 64).astype(jnp.int32) == par
    top = jnp.full((64, 128), par, jnp.int32) == 0

    @pl.when(jnp.logical_not(interior))
    def _():
        for k, d in enumerate(DIRECTIONS):

            @pl.when(jnp.logical_not(inside[d]))
            def _():
                if k < 4:
                    face_in[k] = jnp.zeros((64, 896), BF16)
                else:
                    first_in[k - 4] = jnp.zeros((64, 256), BF16)
                    rest_in[k - 4] = jnp.zeros((64, 384), BF16)
                for c, (sx, sy) in enumerate(CORNERS):
                    if d == (sx, 0):
                        raw_x[c] = jnp.zeros((3, 128, 128), BF16)
                    if d == (0, sy):
                        raw_y[c] = jnp.zeros((3, 128, 128), BF16)

    def place(x, y, z, fact):
        return FACTS * (4 * x + 2 * y + z) + fact

    for copy in scalar_loads:
        copy.wait()
    for c, (sx, sy) in enumerate(CORNERS):
        x, y = (sx + 1) // 2, (sy + 1) // 2
        ix, iy, ox, oy = slots(sx, sy)
        for z in range(2):
            mz = 6 if z == 0 else 5
            mine = agg[x, y, z]
            facts[place(x, y, z, 0)] = mine
            for fact, m, target in (
                (1, mz, agg[x, y, 1 - z]), (2, ix, agg[1 - x, y, z]), (3, iy, agg[x, 1 - y, z]), (4, ox, mine), (5, oy, mine)
            ):
                facts[place(x, y, z, fact)] = jnp.where(links[x, y, z, m - 1] == 1, target, NOWHERE)

    def pack(evens_first):
        for c, (sx, sy) in enumerate(CORNERS):
            x, y = (sx + 1) // 2, (sy + 1) // 2
            ix, iy, ox, oy = slots(sx, sy)
            p_loads[c].wait()
            for z in range(2):
                for j, (m, n) in enumerate(((0, 6 if z == 0 else 5), (ix, iy), (ox, oy))):
                    pair = [p_v[x, y, z, m], p_v[x, y, z, n]]
                    raw[c, j, 64 * z : 64 * z + 64, :] = jnp.concatenate(pair if evens_first else pair[::-1], axis=1)

    pl.when(par == 0)(lambda: pack(True))
    pl.when(par == 1)(lambda: pack(False))

    pl.semaphore_wait(barrier, sum(there.astype(jnp.int32) for there in inside.values()))

    facts_copies = {}
    for k, (dx, dy) in enumerate(DIRECTIONS):
        facts_copies[dx, dy] = remote(facts, facts_in.at[k], (facts_s, facts_r), k, (-dx, -dy))
    copies_x, copies_y = [], []
    for c, (sx, sy) in enumerate(CORNERS):
        copies_x.append(remote(raw.at[corner(-sx, sy)], raw_x.at[c], (raw_s, raw_r), c, (-sx, 0)))
        copies_y.append(remote(raw.at[corner(sx, -sy)], raw_y.at[c], (raw_s, raw_r), 4 + c, (0, -sy)))
    each(
        [((-dx, -dy), facts_copies[dx, dy].start) for dx, dy in CORNERS + FACES]
        + [((0, -sy), copies_y[c].start) for c, (sx, sy) in enumerate(CORNERS)]
        + [((-sx, 0), copies_x[c].start) for c, (sx, sy) in enumerate(CORNERS)]
    )

    for c, (sx, sy) in enumerate(CORNERS):
        x, y = (sx + 1) // 2, (sy + 1) // 2
        a_loads[c].wait()

        def block(z, m):
            value = a_v[x, y, z, m]
            if m == 0:
                return value
            return (value.astype(F32) * links[x, y, z, m - 1].astype(F32)).astype(BF16)

        mats[c, 0, 0:64, :] = jnp.concatenate([block(0, 0), block(0, 6)], axis=1)
        mats[c, 0, 64:128, :] = jnp.concatenate([block(1, 5), block(1, 0)], axis=1)
        zero = jnp.zeros((64, 64), BF16)
        for k, m in enumerate(slots(sx, sy)):
            mats[c, k + 1, 0:64, :] = jnp.concatenate([block(0, m), zero], axis=1)
            mats[c, k + 1, 64:128, :] = jnp.concatenate([zero, block(1, m)], axis=1)

    def told(d, x, y, z, fact):
        return jnp.where(inside[d], facts_in[DIRECTIONS.index(d), place(x, y, z, fact)], NOWHERE)

    def combine(source, target, names, flipped, origin, targets):
        def lane_ids(pair):
            first, second = (((mx + origin[0] + t[0]) * ny + my + origin[1] + t[1]) for t in pair)
            return jnp.where(even_row, second, first) if flipped else jnp.where(even_row, first, second)

        ids = [lane_ids(pair) for pair in names]
        swapped = [lane_ids(pair[::-1]) for pair in names]
        evens = jnp.logical_not(even_row) if flipped else even_row
        for z in range(2):
            rows = slice(64 * z, 64 * z + 64)
            boxes = targets(z)
            values = [source[j, rows, :].astype(F32) for j in range(3)]
            lanes = [jnp.where(evens, boxes[2 * j], boxes[2 * j + 1]) for j in range(3)]

            def picked(names, which):
                return sum(values[j] * (lanes[j] == names).astype(F32) for j in which)

            target[0, rows, :] = (
                picked(ids[0], (0, 1, 2)) + pltpu.roll(picked(swapped[0], (0, 1, 2)), 64, 1)
            ).astype(BF16)
            target[1, rows, :] = (picked(ids[1], (0, 2)) + pltpu.roll(picked(swapped[1], (0, 1)), 64, 1)).astype(BF16)
            target[2, rows, :] = picked(ids[2], (1,)).astype(BF16)

    each([(d, facts_copies[d].wait_recv) for d in DIRECTIONS])
    for c, (sx, sy) in enumerate(CORNERS):
        x, y = (sx + 1) // 2, (sy + 1) // 2
        combine(
            raw.at[c], tiles.at[c], element_tiles(sx, sy), False, (0, 0),
            lambda z: [facts[place(x, y, z, fact)] for fact in range(4)]
            + [told((sx, 0), 1 - x, y, z, 4), told((0, sy), x, 1 - y, z, 5)],
        )

    for c, (sx, sy) in enumerate(CORNERS):
        blocks = {}
        for t, pair in enumerate(element_tiles(sx, sy)):
            turned = tiles[c, t].astype(F32).T
            blocks[pair[0]] = jnp.where(top, turned[0:64], turned[64:128]).astype(BF16)
            blocks[pair[1]] = jnp.where(top, turned[64:128], turned[0:64]).astype(BF16)
        ptd[c] = blocks[sx, sy]
        for r, offset in enumerate(FACES + ((0, 0),)):
            ptg[64 * r : 64 * r + 64, 128 * c : 128 * c + 128] = blocks[offset]

    def product(mat, ref, c):
        rows = dot(mat, jnp.concatenate([ref[c, 0], ref[c, 1], ref[c, 2]], axis=1))
        return rows[:, 0:128], rows[:, 128:256], rows[:, 256:384]

    nothing = jnp.zeros((128, 128), F32)
    for c, (sx, sy) in enumerate(CORNERS):
        s0, s1, s2 = product(mats[c, 0], tiles, c)
        x0, x1, x2 = product(mats[c, 1], tiles, corner(-sx, sy))
        y0, y1, y2 = product(mats[c, 2], tiles, corner(sx, -sy))
        im[c, 0] = s0 + jnp.where(even, x0 + y0, nothing)
        im[c, 1] = s1 + jnp.where(even, x2 + y1, x1 + y2)
        im[c, 2] = s2 + jnp.where(even, x1 + y2, x2 + y1)
        im[c, 3] = jnp.where(even, nothing, y0)
        im[c, 4] = jnp.where(even, nothing, x0)

    for jx in range(7):
        for jy in range(7):
            if abs(jx - 3) + abs(jy - 3) > 3:
                out[0, 0, jx, jy] = jnp.zeros((64, 64), BF16)

    each([((sx, 0), copies_x[c].wait_recv) for c, (sx, sy) in enumerate(CORNERS)])
    for c, (sx, sy) in enumerate(CORNERS):
        x, y = (sx + 1) // 2, (sy + 1) // 2
        combine(
            raw_x.at[c], tiles_x.at[c], element_tiles(-sx, sy), False, (sx, 0),
            lambda z: [told((sx, 0), 1 - x, y, z, fact) for fact in range(4)]
            + [facts[place(x, y, z, 4)], told((sx, sy), 1 - x, 1 - y, z, 5)],
        )
    for c in range(4):
        x0, x1, x2 = product(mats[c, 3], tiles_x, c)
        im[c, 0] += x1
        im[c, 1] += x0
        im[c, 3] += x2
    for c in range(4):
        first = jnp.concatenate([im[c, 2].astype(BF16), im[c, 3].astype(BF16)], axis=1)
        first_out[c] = dot(ptd[c], first).astype(BF16)
    first_copies = [
        remote(first_out.at[corner(-sx, -sy)], first_in.at[c], (first_s, first_r), c, (-sx, -sy))
        for c, (sx, sy) in enumerate(CORNERS)
    ]
    each([((-sx, -sy), first_copies[c].start) for c, (sx, sy) in enumerate(CORNERS)])

    rest_copies = [
        remote(rest_out.at[corner(-sx, -sy)], rest_in.at[c], (rest_s, rest_r), c, (-sx, -sy))
        for c, (sx, sy) in enumerate(CORNERS)
    ]
    for group in ((0, 1), (2, 3)):
        each([((0, CORNERS[c][1]), copies_y[c].wait_recv) for c in group])
        for c in group:
            sx, sy = CORNERS[c]
            x, y = (sx + 1) // 2, (sy + 1) // 2
            combine(
                raw_y.at[c], tiles_y.at[c], element_tiles(sx, -sy), True, (0, sy),
                lambda z: [told((0, sy), x, 1 - y, z, fact) for fact in range(4)]
                + [told((sx, sy), 1 - x, 1 - y, z, 4), facts[place(x, y, z, 5)]],
            )
        for c in group:
            sx, sy = CORNERS[c]
            y0, y1, y2 = product(mats[c, 4], tiles_y, c)
            image = [im[c, 0] + y1, im[c, 1] + y0, im[c, 2], im[c, 3], im[c, 4] + y2]
            rest = jnp.concatenate([image[0].astype(BF16), image[1].astype(BF16), image[4].astype(BF16)], axis=1)
            rest_out[c] = dot(ptd[c], rest).astype(BF16)
            names = image_tiles(sx, sy)
            at_even = {pair[0]: i for i, pair in enumerate(names)}
            at_odd = {pair[1]: i for i, pair in enumerate(names)}
            for g, (e, o) in enumerate(PAIRS):
                evens = image[at_even[e]] if e in at_even else nothing
                odds = image[at_odd[o]] if o in at_odd else nothing
                imw[128 * c : 128 * c + 128, 128 * g : 128 * g + 128] = jnp.where(even, evens, odds).astype(BF16)
        each([(CORNERS[c], rest_copies[3 - c].start) for c in group])

    wide = imw[...]
    face_copies = [
        remote(face_out.at[FACES.index((-dx, -dy))], face_in.at[k], (face_s, face_r), k, (-dx, -dy))
        for k, (dx, dy) in enumerate(FACES)
    ]
    for first in (2, 0):
        rows = dot(ptg[64 * first : 64 * first + 128, :], wide).astype(BF16)
        face_out[first] = rows[0:64]
        face_out[first + 1] = rows[64:128]
        each([((-FACES[k][0], -FACES[k][1]), face_copies[k].start) for k in (first, first + 1)])

    offsets = [(dx, dy) for dx in range(-3, 4) for dy in range(-3, 4) if abs(dx) + abs(dy) <= 3]
    at = {offset: i for i, offset in enumerate(offsets)}

    def tiles_of(ref, names, d):
        return [
            (add(offset, d), ref, g) for g, pair in enumerate(names) for offset in pair if offset is not None
        ]

    own = dot(ptg[256:320, :], wide)
    mine = {offset: g for g, pair in enumerate(PAIRS) for offset in pair if offset is not None}
    early = [source for k in (0, 1) for source in tiles_of(face_in.at[k], PAIRS, FACES[k])]
    late = []
    for c, (sx, sy) in enumerate(CORNERS):
        names = image_tiles(-sx, -sy)
        early.extend(tiles_of(first_in.at[c], names[2:4], (sx, sy)))
        late.extend(tiles_of(rest_in.at[c], (names[0], names[1], names[4]), (sx, sy)))

    def gathered(total, offset, sources):
        for name, ref, g in sources:
            if name == offset:
                tile = ref[:, 128 * g : 128 * g + 128].astype(F32)
                total = tile if total is None else total + tile
        return jnp.zeros((64, 128), F32) if total is None else total

    each(
        [((sx, sy), first_copies[c].wait_recv) for c, (sx, sy) in enumerate(CORNERS)]
        + [(FACES[k], face_copies[k].wait_recv) for k in (0, 1)]
    )
    for offset in offsets:
        g = mine.get(offset)
        acc[at[offset]] = gathered(None if g is None else own[:, 128 * g : 128 * g + 128], offset, early)
    each([((sx, sy), rest_copies[c].wait_recv) for c, (sx, sy) in enumerate(CORNERS)])

    def finish(evens_first):
        def on_left(value, offset):
            return value if (offset[1] % 2 == 0) == evens_first else pltpu.roll(value, 64, 1)

        def put(offset, value):
            out[0, 0, offset[0] + 3, offset[1] + 3] = value[:, 0:64].astype(BF16)

        last = {}
        for k in (2, 3):
            for g, pair in enumerate(PAIRS):
                for offset in pair:
                    if offset is not None:
                        last.setdefault(add(offset, FACES[k]), []).append((k, g))
        for offset in offsets:
            value = on_left(gathered(acc[at[offset]], offset, late), offset)
            if offset in last:
                acc[at[offset]] = value
            else:
                put(offset, value)
        each([(FACES[k], face_copies[k].wait_recv) for k in (2, 3)])
        for offset in offsets:
            if offset in last:
                value = acc[at[offset]]
                for k, g in last[offset]:
                    value += on_left(face_in[k, :, 128 * g : 128 * g + 128].astype(F32), offset)
                put(offset, value)

    pl.when(par == 0)(lambda: finish(True))
    pl.when(par == 1)(lambda: finish(False))

    each(
        [((-dx, -dy), facts_copies[dx, dy].wait_send) for dx, dy in DIRECTIONS]
        + [((-dx, -dy), face_copies[k].wait_send) for k, (dx, dy) in enumerate(FACES)]
        + [((-sx, 0), copies_x[c].wait_send) for c, (sx, sy) in enumerate(CORNERS)]
        + [((0, -sy), copies_y[c].wait_send) for c, (sx, sy) in enumerate(CORNERS)]
        + [((-sx, -sy), first_copies[c].wait_send) for c, (sx, sy) in enumerate(CORNERS)]
        + [((-sx, -sy), rest_copies[c].wait_send) for c, (sx, sy) in enumerate(CORNERS)]
    )


def per_device(fine_matrix, prolongator, aggregate, face_links):
    nx, ny = lax.axis_size("sx"), lax.axis_size("sy")
    dma = pltpu.SemaphoreType.DMA
    return pl.pallas_call(
        functools.partial(kernel, nx, ny),
        out_shape=jax.ShapeDtypeStruct((1, 1, 7, 7, 64, 64), BF16),
        in_specs=[pl.BlockSpec(memory_space=pl.ANY)] * 4,
        out_specs=pl.BlockSpec(memory_space=pltpu.VMEM),
        scratch_shapes=[
            pltpu.VMEM((2, 2, 2, 7, 64, 64), BF16),
            pltpu.VMEM((2, 2, 2, 7, 64, 64), BF16),
            pltpu.SMEM((2, 2, 2), jnp.int32),
            pltpu.SMEM((2, 2, 2, 6), jnp.int32),
            pltpu.SMEM((64,), jnp.int32),
            pltpu.SMEM((8, 64), jnp.int32),
            *[pltpu.VMEM((4, 3, 128, 128), BF16)] * 6,
            pltpu.VMEM((4, 5, 128, 128), BF16),
            pltpu.VMEM((4, 5, 128, 128), F32),
            pltpu.VMEM((320, 512), BF16),
            pltpu.VMEM((4, 64, 128), BF16),
            pltpu.VMEM((512, 896), BF16),
            *[pltpu.VMEM((4, 64, 896), BF16)] * 2,
            *[pltpu.VMEM((4, 64, 256), BF16)] * 2,
            *[pltpu.VMEM((4, 64, 384), BF16)] * 2,
            pltpu.VMEM((25, 64, 128), F32),
            dma((2,)),
            dma((4,)),
            dma((4,)),
            *[dma((8,))] * 4,
            *[dma((4,))] * 6,
        ],
        compiler_params=pltpu.CompilerParams(
            collective_id=0, has_side_effects=True, vmem_limit_bytes=32 * 1024 * 1024
        ),
        name="galerkin",
    )(*(pltpu.with_memory_space_constraint(v, pltpu.HBM) for v in (fine_matrix, prolongator, aggregate, face_links)))


def solution(mesh):
    return jax.shard_map(
        per_device,
        mesh=mesh,
        in_specs=(
            P("sx", "sy", None, None, None, None),
            P("sx", "sy", None, None, None, None),
            P("sx", "sy", None),
            P("sx", "sy", None, None),
        ),
        out_specs=P("sx", "sy", None, None, None, None),
        check_vma=False,
    )
```

```python
import functools

import jax
import jax.numpy as jnp
from jax import lax
from jax.experimental import pallas as pl
from jax.experimental.pallas import tpu as pltpu
from jax.sharding import PartitionSpec as P

MESH = pl.DeviceIdType.MESH
F32 = jnp.float32
BF16 = jnp.bfloat16

CORNERS = ((-1, -1), (-1, 1), (1, -1), (1, 1))
FACES = ((-1, 0), (1, 0), (0, -1), (0, 1))
DIRECTIONS = FACES + CORNERS
NOWHERE = -1000000
FACTS = 6

EVENS = ((0, 0), (-1, 0), (1, 0), (-2, 0), (2, 0), (0, -2), (0, 2))
ODDS = ((0, -1), (0, 1), (-1, -1), (-1, 1), (1, -1), (1, 1), None)
PAIRS = tuple(zip(EVENS, ODDS))


def corner(sx, sy):
    return (2 if sx > 0 else 0) + (1 if sy > 0 else 0)


def element_tiles(sx, sy):
    return (((0, 0), (sx, sy)), ((sx, 0), (0, sy)), ((-sx, 0), (0, -sy)))


def image_tiles(sx, sy):
    return element_tiles(sx, sy) + (((2 * sx, 0), (sx, -sy)), ((0, 2 * sy), (-sx, sy)))


def slots(sx, sy):
    return (2 if sx < 0 else 1), (4 if sy < 0 else 3), (1 if sx < 0 else 2), (3 if sy < 0 else 4)


def add(u, v):
    return (u[0] + v[0], u[1] + v[1])


def dot(a, b):
    return jnp.dot(a, b, preferred_element_type=F32)


def kernel(
    nx, ny, a_hbm, p_hbm, agg_hbm, links_hbm, out,
    a_v, p_v, agg, links, facts, facts_in, raw, raw_x, raw_y, tiles, tiles_x, tiles_y, mats, im, ptg, ptd, imw,
    face_out, face_in, first_out, first_in, rest_out, rest_in, acc,
    scalar_sem, p_sem, a_sem, facts_s, facts_r, raw_s, raw_r, face_s, face_r, first_s, first_r, rest_s, rest_r,
):
    mx, my = lax.axis_index("sx"), lax.axis_index("sy")
    par = lax.rem(my, 2)

    def device(dx, dy):
        return (lax.rem(mx + dx + nx, nx), lax.rem(my + dy + ny, ny))

    inside = {(-1, 0): mx > 0, (1, 0): mx < nx - 1, (0, -1): my > 0, (0, 1): my < ny - 1}
    for sx, sy in CORNERS:
        inside[sx, sy] = jnp.logical_and(inside[sx, 0], inside[0, sy])

    interior = jnp.logical_and(
        jnp.logical_and(inside[-1, 0], inside[1, 0]), jnp.logical_and(inside[0, -1], inside[0, 1])
    )

    def each(actions):
        @pl.when(interior)
        def _():
            for _, action in actions:
                action()

        @pl.when(jnp.logical_not(interior))
        def _():
            for d, action in actions:
                pl.when(inside[d])(action)

    def remote(src, dst, sems, k, d):
        return pltpu.make_async_remote_copy(
            src_ref=src, dst_ref=dst, send_sem=sems[0].at[k], recv_sem=sems[1].at[k],
            device_id=device(*d), device_id_type=MESH,
        )

    barrier = pltpu.get_barrier_semaphore()
    def greet(d):
        return d, lambda: pl.semaphore_signal(barrier, inc=1, device_id=device(*d), device_id_type=MESH)

    each([greet(d) for d in DIRECTIONS])
    scalar_loads = (
        pltpu.make_async_copy(agg_hbm, agg, scalar_sem.at[0]),
        pltpu.make_async_copy(links_hbm, links, scalar_sem.at[1]),
    )
    p_loads, a_loads = [], []
    for c, (sx, sy) in enumerate(CORNERS):
        x, y = (sx + 1) // 2, (sy + 1) // 2
        p_loads.append(pltpu.make_async_copy(p_hbm.at[x, y], p_v.at[x, y], p_sem.at[c]))
        a_loads.append(pltpu.make_async_copy(a_hbm.at[x, y], a_v.at[x, y], a_sem.at[c]))
    for copy in (*scalar_loads, *p_loads, *a_loads):
        copy.start()

    even_row = (lax.broadcasted_iota(jnp.int32, (1, 128), 1) >= 64).astype(jnp.int32) == par
    even = (lax.broadcasted_iota(jnp.int32, (128, 128), 1) >= 64).astype(jnp.int32) == par
    top = jnp.full((64, 128), par, jnp.int32) == 0

    @pl.when(jnp.logical_not(interior))
    def _():
        for k, d in enumerate(DIRECTIONS):

            @pl.when(jnp.logical_not(inside[d]))
            def _():
                if k < 4:
                    face_in[k] = jnp.zeros((64, 896), BF16)
                else:
                    rest_in[k - 4] = jnp.zeros((64, 384), BF16)
                for c, (sx, sy) in enumerate(CORNERS):
                    if d == (sx, 0):
                        raw_x[c] = jnp.zeros((3, 128, 128), BF16)
                        first_in[c] = jnp.zeros((64, 256), BF16)
                    if d == (0, sy):
                        raw_y[c] = jnp.zeros((3, 128, 128), BF16)

    def place(x, y, z, fact):
        return FACTS * (4 * x + 2 * y + z) + fact

    for copy in scalar_loads:
        copy.wait()
    for c, (sx, sy) in enumerate(CORNERS):
        x, y = (sx + 1) // 2, (sy + 1) // 2
        ix, iy, ox, oy = slots(sx, sy)
        for z in range(2):
            mz = 6 if z == 0 else 5
            mine = agg[x, y, z]
            facts[place(x, y, z, 0)] = mine
            for fact, m, target in (
                (1, mz, agg[x, y, 1 - z]), (2, ix, agg[1 - x, y, z]), (3, iy, agg[x, 1 - y, z]), (4, ox, mine), (5, oy, mine)
            ):
                facts[place(x, y, z, fact)] = jnp.where(links[x, y, z, m - 1] == 1, target, NOWHERE)

    def pack(evens_first):
        for c, (sx, sy) in enumerate(CORNERS):
            x, y = (sx + 1) // 2, (sy + 1) // 2
            ix, iy, ox, oy = slots(sx, sy)
            p_loads[c].wait()
            for z in range(2):
                for j, (m, n) in enumerate(((0, 6 if z == 0 else 5), (ix, iy), (ox, oy))):
                    pair = [p_v[x, y, z, m], p_v[x, y, z, n]]
                    raw[c, j, 64 * z : 64 * z + 64, :] = jnp.concatenate(pair if evens_first else pair[::-1], axis=1)

    pl.when(par == 0)(lambda: pack(True))
    pl.when(par == 1)(lambda: pack(False))

    pl.semaphore_wait(barrier, sum(there.astype(jnp.int32) for there in inside.values()))

    facts_copies = {}
    for k, (dx, dy) in enumerate(DIRECTIONS):
        facts_copies[dx, dy] = remote(facts, facts_in.at[k], (facts_s, facts_r), k, (-dx, -dy))
    copies_x, copies_y = [], []
    for c, (sx, sy) in enumerate(CORNERS):
        copies_x.append(remote(raw.at[corner(-sx, sy)], raw_x.at[c], (raw_s, raw_r), c, (-sx, 0)))
        copies_y.append(remote(raw.at[corner(sx, -sy)], raw_y.at[c], (raw_s, raw_r), 4 + c, (0, -sy)))
    each(
        [((-dx, -dy), facts_copies[dx, dy].start) for dx, dy in CORNERS + FACES]
        + [((0, -sy), copies_y[c].start) for c, (sx, sy) in enumerate(CORNERS)]
        + [((-sx, 0), copies_x[c].start) for c, (sx, sy) in enumerate(CORNERS)]
    )

    for c, (sx, sy) in enumerate(CORNERS):
        x, y = (sx + 1) // 2, (sy + 1) // 2
        a_loads[c].wait()

        def block(z, m):
            value = a_v[x, y, z, m]
            if m == 0:
                return value
            return (value.astype(F32) * links[x, y, z, m - 1].astype(F32)).astype(BF16)

        mats[c, 0, 0:64, :] = jnp.concatenate([block(0, 0), block(0, 6)], axis=1)
        mats[c, 0, 64:128, :] = jnp.concatenate([block(1, 5), block(1, 0)], axis=1)
        zero = jnp.zeros((64, 64), BF16)
        for k, m in enumerate(slots(sx, sy)):
            mats[c, k + 1, 0:64, :] = jnp.concatenate([block(0, m), zero], axis=1)
            mats[c, k + 1, 64:128, :] = jnp.concatenate([zero, block(1, m)], axis=1)

    def told(d, x, y, z, fact):
        return jnp.where(inside[d], facts_in[DIRECTIONS.index(d), place(x, y, z, fact)], NOWHERE)

    def combine(source, target, names, flipped, origin, targets):
        def lane_ids(pair):
            first, second = (((mx + origin[0] + t[0]) * ny + my + origin[1] + t[1]) for t in pair)
            return jnp.where(even_row, second, first) if flipped else jnp.where(even_row, first, second)

        ids = [lane_ids(pair) for pair in names]
        swapped = [lane_ids(pair[::-1]) for pair in names]
        evens = jnp.logical_not(even_row) if flipped else even_row
        for z in range(2):
            rows = slice(64 * z, 64 * z + 64)
            boxes = targets(z)
            values = [source[j, rows, :].astype(F32) for j in range(3)]
            lanes = [jnp.where(evens, boxes[2 * j], boxes[2 * j + 1]) for j in range(3)]

            def picked(names, which):
                return sum(values[j] * (lanes[j] == names).astype(F32) for j in which)

            target[0, rows, :] = (
                picked(ids[0], (0, 1, 2)) + pltpu.roll(picked(swapped[0], (0, 1, 2)), 64, 1)
            ).astype(BF16)
            target[1, rows, :] = (picked(ids[1], (0, 2)) + pltpu.roll(picked(swapped[1], (0, 1)), 64, 1)).astype(BF16)
            target[2, rows, :] = picked(ids[2], (1,)).astype(BF16)

    each([(d, facts_copies[d].wait_recv) for d in FACES])
    for c, (sx, sy) in enumerate(CORNERS):
        x, y = (sx + 1) // 2, (sy + 1) // 2
        combine(
            raw.at[c], tiles.at[c], element_tiles(sx, sy), False, (0, 0),
            lambda z: [facts[place(x, y, z, fact)] for fact in range(4)]
            + [told((sx, 0), 1 - x, y, z, 4), told((0, sy), x, 1 - y, z, 5)],
        )

    for c, (sx, sy) in enumerate(CORNERS):
        blocks = {}
        for t, pair in enumerate(element_tiles(sx, sy)):
            turned = tiles[c, t].astype(F32).T
            blocks[pair[0]] = jnp.where(top, turned[0:64], turned[64:128]).astype(BF16)
            blocks[pair[1]] = jnp.where(top, turned[64:128], turned[0:64]).astype(BF16)
        ptd[c] = blocks[sx, sy]
        for r, offset in enumerate(FACES + ((0, 0),)):
            ptg[64 * r : 64 * r + 64, 128 * c : 128 * c + 128] = blocks[offset]

    def product(mat, ref, c):
        rows = dot(mat, jnp.concatenate([ref[c, 0], ref[c, 1], ref[c, 2]], axis=1))
        return rows[:, 0:128], rows[:, 128:256], rows[:, 256:384]

    nothing = jnp.zeros((128, 128), F32)
    for c, (sx, sy) in enumerate(CORNERS):
        s0, s1, s2 = product(mats[c, 0], tiles, c)
        x0, x1, x2 = product(mats[c, 1], tiles, corner(-sx, sy))
        y0, y1, y2 = product(mats[c, 2], tiles, corner(sx, -sy))
        im[c, 0] = s0 + jnp.where(even, x0 + y0, nothing)
        im[c, 1] = s1 + jnp.where(even, x2 + y1, x1 + y2)
        im[c, 2] = s2 + jnp.where(even, x1 + y2, x2 + y1)
        im[c, 3] = jnp.where(even, nothing, y0)
        im[c, 4] = jnp.where(even, nothing, x0)

    for jx in range(7):
        for jy in range(7):
            if abs(jx - 3) + abs(jy - 3) > 3:
                out[0, 0, jx, jy] = jnp.zeros((64, 64), BF16)

    each(
        [(d, facts_copies[d].wait_recv) for d in CORNERS]
        + [((sx, 0), copies_x[c].wait_recv) for c, (sx, sy) in enumerate(CORNERS)]
    )
    for c, (sx, sy) in enumerate(CORNERS):
        x, y = (sx + 1) // 2, (sy + 1) // 2
        combine(
            raw_x.at[c], tiles_x.at[c], element_tiles(-sx, sy), False, (sx, 0),
            lambda z: [told((sx, 0), 1 - x, y, z, fact) for fact in range(4)]
            + [facts[place(x, y, z, 4)], told((sx, sy), 1 - x, 1 - y, z, 5)],
        )
    for c in range(4):
        x0, x1, x2 = product(mats[c, 3], tiles_x, c)
        im[c, 0] += x1
        im[c, 1] += x0
        im[c, 3] += x2
    for c in range(4):
        first = jnp.concatenate([im[c, 2].astype(BF16), im[c, 3].astype(BF16)], axis=1)
        first_out[c] = dot(ptd[c], first).astype(BF16)
    first_copies = [
        remote(first_out.at[corner(-sx, sy)], first_in.at[c], (first_s, first_r), c, (-sx, 0))
        for c, (sx, sy) in enumerate(CORNERS)
    ]
    each([((-sx, 0), first_copies[c].start) for c, (sx, sy) in enumerate(CORNERS)])

    rest_copies = [
        remote(rest_out.at[corner(-sx, -sy)], rest_in.at[c], (rest_s, rest_r), c, (-sx, -sy))
        for c, (sx, sy) in enumerate(CORNERS)
    ]
    for group in ((0,), (1,), (2,), (3,)):
        each([((0, CORNERS[c][1]), copies_y[c].wait_recv) for c in group])
        for c in group:
            sx, sy = CORNERS[c]
            x, y = (sx + 1) // 2, (sy + 1) // 2
            combine(
                raw_y.at[c], tiles_y.at[c], element_tiles(sx, -sy), True, (0, sy),
                lambda z: [told((0, sy), x, 1 - y, z, fact) for fact in range(4)]
                + [told((sx, sy), 1 - x, 1 - y, z, 4), facts[place(x, y, z, 5)]],
            )
        for c in group:
            sx, sy = CORNERS[c]
            y0, y1, y2 = product(mats[c, 4], tiles_y, c)
            image = [im[c, 0] + y1, im[c, 1] + y0, im[c, 2], im[c, 3], im[c, 4] + y2]
            rest = jnp.concatenate([image[0].astype(BF16), image[1].astype(BF16), image[4].astype(BF16)], axis=1)
            rest_out[c] = dot(ptd[c], rest).astype(BF16)
            names = image_tiles(sx, sy)
            at_even = {pair[0]: i for i, pair in enumerate(names)}
            at_odd = {pair[1]: i for i, pair in enumerate(names)}
            for g, (e, o) in enumerate(PAIRS):
                evens = image[at_even[e]] if e in at_even else nothing
                odds = image[at_odd[o]] if o in at_odd else nothing
                imw[128 * c : 128 * c + 128, 128 * g : 128 * g + 128] = jnp.where(even, evens, odds).astype(BF16)
        each([(CORNERS[c], rest_copies[3 - c].start) for c in group])

    each([((sx, 0), first_copies[c].wait_recv) for c, (sx, sy) in enumerate(CORNERS)])
    passed = {}
    for c, (sx, sy) in enumerate(CORNERS):
        for i, pair in enumerate(image_tiles(-sx, sy)[2:4]):
            tile = first_in[c, :, 128 * i : 128 * i + 128].astype(F32)
            for side, offset in enumerate(pair):
                g = (EVENS, ODDS)[side].index(add(offset, (sx, 0)))
                key = (sy, g, side)
                passed[key] = tile if key not in passed else passed[key] + tile

    def with_passed(tile, sy, g):
        halves = [passed.get((sy, g, side)) for side in range(2)]
        if halves == [None, None]:
            return tile
        halves = [nothing[0:64] if half is None else half for half in halves]
        return tile + jnp.where(even[0:64], *halves)

    wide = imw[...]
    face_copies = [
        remote(face_out.at[FACES.index((-dx, -dy))], face_in.at[k], (face_s, face_r), k, (-dx, -dy))
        for k, (dx, dy) in enumerate(FACES)
    ]
    for first in (2, 0):
        rows = dot(ptg[64 * first : 64 * first + 128, :], wide)
        for k in (first, first + 1):
            for g in range(len(PAIRS)):
                tile = rows[64 * (k - first) : 64 * (k - first) + 64, 128 * g : 128 * g + 128]
                if first == 2:
                    tile = with_passed(tile, FACES[k][1], g)
                face_out[k, :, 128 * g : 128 * g + 128] = tile.astype(BF16)
        each([((-FACES[k][0], -FACES[k][1]), face_copies[k].start) for k in (first, first + 1)])

    offsets = [(dx, dy) for dx in range(-3, 4) for dy in range(-3, 4) if abs(dx) + abs(dy) <= 3]
    at = {offset: i for i, offset in enumerate(offsets)}

    def tiles_of(ref, names, d):
        return [
            (add(offset, d), ref, g) for g, pair in enumerate(names) for offset in pair if offset is not None
        ]

    own = dot(ptg[256:320, :], wide)
    mine = {offset: g for g, pair in enumerate(PAIRS) for offset in pair if offset is not None}
    early = [source for k in (0, 1) for source in tiles_of(face_in.at[k], PAIRS, FACES[k])]
    late = []
    for c, (sx, sy) in enumerate(CORNERS):
        names = image_tiles(-sx, -sy)
        late.extend(tiles_of(rest_in.at[c], (names[0], names[1], names[4]), (sx, sy)))

    def gathered(total, offset, sources):
        for name, ref, g in sources:
            if name == offset:
                tile = ref[:, 128 * g : 128 * g + 128].astype(F32)
                total = tile if total is None else total + tile
        return jnp.zeros((64, 128), F32) if total is None else total

    each([(FACES[k], face_copies[k].wait_recv) for k in (0, 1)])
    for offset in offsets:
        g = mine.get(offset)
        acc[at[offset]] = gathered(None if g is None else own[:, 128 * g : 128 * g + 128], offset, early)
    each(
        [((-dx, -dy), facts_copies[dx, dy].wait_send) for dx, dy in DIRECTIONS]
        + [((-sx, 0), copies_x[c].wait_send) for c, (sx, sy) in enumerate(CORNERS)]
        + [((0, -sy), copies_y[c].wait_send) for c, (sx, sy) in enumerate(CORNERS)]
        + [((-sx, 0), first_copies[c].wait_send) for c, (sx, sy) in enumerate(CORNERS)]
        + [((sx, sy), rest_copies[c].wait_recv) for c, (sx, sy) in enumerate(CORNERS)]
    )

    def finish(evens_first):
        def on_left(value, offset):
            return value if (offset[1] % 2 == 0) == evens_first else pltpu.roll(value, 64, 1)

        def put(offset, value):
            out[0, 0, offset[0] + 3, offset[1] + 3] = value[:, 0:64].astype(BF16)

        last = {}
        for k in (2, 3):
            for g, pair in enumerate(PAIRS):
                for offset in pair:
                    if offset is not None:
                        last.setdefault(add(offset, FACES[k]), []).append((k, g))
        for offset in offsets:
            value = on_left(gathered(acc[at[offset]], offset, late), offset)
            if offset in last:
                acc[at[offset]] = value
            else:
                put(offset, value)
        each(
            [((-sx, -sy), rest_copies[c].wait_send) for c, (sx, sy) in enumerate(CORNERS)]
            + [((-FACES[k][0], -FACES[k][1]), face_copies[k].wait_send) for k in (0, 1)]
            + [(FACES[k], face_copies[k].wait_recv) for k in (2, 3)]
        )
        for offset in offsets:
            if offset in last:
                value = acc[at[offset]]
                for k, g in last[offset]:
                    value += on_left(face_in[k, :, 128 * g : 128 * g + 128].astype(F32), offset)
                put(offset, value)

    pl.when(par == 0)(lambda: finish(True))
    pl.when(par == 1)(lambda: finish(False))

    each([((-FACES[k][0], -FACES[k][1]), face_copies[k].wait_send) for k in (2, 3)])


def per_device(fine_matrix, prolongator, aggregate, face_links):
    nx, ny = lax.axis_size("sx"), lax.axis_size("sy")
    dma = pltpu.SemaphoreType.DMA
    return pl.pallas_call(
        functools.partial(kernel, nx, ny),
        out_shape=jax.ShapeDtypeStruct((1, 1, 7, 7, 64, 64), BF16),
        in_specs=[pl.BlockSpec(memory_space=pl.ANY)] * 4,
        out_specs=pl.BlockSpec(memory_space=pltpu.VMEM),
        scratch_shapes=[
            pltpu.VMEM((2, 2, 2, 7, 64, 64), BF16),
            pltpu.VMEM((2, 2, 2, 7, 64, 64), BF16),
            pltpu.SMEM((2, 2, 2), jnp.int32),
            pltpu.SMEM((2, 2, 2, 6), jnp.int32),
            pltpu.SMEM((64,), jnp.int32),
            pltpu.SMEM((8, 64), jnp.int32),
            *[pltpu.VMEM((4, 3, 128, 128), BF16)] * 6,
            pltpu.VMEM((4, 5, 128, 128), BF16),
            pltpu.VMEM((4, 5, 128, 128), F32),
            pltpu.VMEM((320, 512), BF16),
            pltpu.VMEM((4, 64, 128), BF16),
            pltpu.VMEM((512, 896), BF16),
            *[pltpu.VMEM((4, 64, 896), BF16)] * 2,
            *[pltpu.VMEM((4, 64, 256), BF16)] * 2,
            *[pltpu.VMEM((4, 64, 384), BF16)] * 2,
            pltpu.VMEM((25, 64, 128), F32),
            dma((2,)),
            dma((4,)),
            dma((4,)),
            *[dma((8,))] * 4,
            *[dma((4,))] * 6,
        ],
        compiler_params=pltpu.CompilerParams(
            collective_id=0, has_side_effects=True, vmem_limit_bytes=32 * 1024 * 1024
        ),
        name="galerkin",
    )(*(pltpu.with_memory_space_constraint(v, pltpu.HBM) for v in (fine_matrix, prolongator, aggregate, face_links)))


def solution(mesh):
    return jax.shard_map(
        per_device,
        mesh=mesh,
        in_specs=(
            P("sx", "sy", None, None, None, None),
            P("sx", "sy", None, None, None, None),
            P("sx", "sy", None),
            P("sx", "sy", None, None),
        ),
        out_specs=P("sx", "sy", None, None, None, None),
        check_vma=False,
    )
```

```python
import functools

import jax
import jax.numpy as jnp
from jax import lax
from jax.experimental import pallas as pl
from jax.experimental.pallas import tpu as pltpu
from jax.sharding import PartitionSpec as P

MESH = pl.DeviceIdType.MESH
F32 = jnp.float32
BF16 = jnp.bfloat16

CORNERS = ((-1, -1), (-1, 1), (1, -1), (1, 1))
FACES = ((-1, 0), (1, 0), (0, -1), (0, 1))
DIRECTIONS = FACES + CORNERS
NOWHERE = -1000000
FACTS = 6

EVENS = ((0, 0), (-1, 0), (1, 0), (-2, 0), (2, 0), (0, -2), (0, 2))
ODDS = ((0, -1), (0, 1), (-1, -1), (-1, 1), (1, -1), (1, 1), None)
PAIRS = tuple(zip(EVENS, ODDS))


def corner(sx, sy):
    return (2 if sx > 0 else 0) + (1 if sy > 0 else 0)


def element_tiles(sx, sy):
    return (((0, 0), (sx, sy)), ((sx, 0), (0, sy)), ((-sx, 0), (0, -sy)))


def image_tiles(sx, sy):
    return element_tiles(sx, sy) + (((2 * sx, 0), (sx, -sy)), ((0, 2 * sy), (-sx, sy)))


def slots(sx, sy):
    return (2 if sx < 0 else 1), (4 if sy < 0 else 3), (1 if sx < 0 else 2), (3 if sy < 0 else 4)


def add(u, v):
    return (u[0] + v[0], u[1] + v[1])


def dot(a, b):
    return jnp.dot(a, b, preferred_element_type=F32)


def kernel(
    nx, ny, a_hbm, p_hbm, agg_hbm, links_hbm, out,
    a_v, p_v, agg, links, facts, facts_in, raw, raw_x, raw_y, tiles, tiles_x, tiles_y, mats, im, ptg, ptd, imw,
    face_out, face_in, first_out, first_in, rest_out, rest_in, acc,
    scalar_sem, p_sem, a_sem, facts_s, facts_r, raw_s, raw_r, face_s, face_r, first_s, first_r, rest_s, rest_r,
):
    mx, my = lax.axis_index("sx"), lax.axis_index("sy")
    par = lax.rem(my, 2)

    def device(dx, dy):
        return (lax.rem(mx + dx + nx, nx), lax.rem(my + dy + ny, ny))

    inside = {(-1, 0): mx > 0, (1, 0): mx < nx - 1, (0, -1): my > 0, (0, 1): my < ny - 1}
    for sx, sy in CORNERS:
        inside[sx, sy] = jnp.logical_and(inside[sx, 0], inside[0, sy])

    interior = jnp.logical_and(
        jnp.logical_and(inside[-1, 0], inside[1, 0]), jnp.logical_and(inside[0, -1], inside[0, 1])
    )

    def each(actions):
        @pl.when(interior)
        def _():
            for _, action in actions:
                action()

        @pl.when(jnp.logical_not(interior))
        def _():
            for d, action in actions:
                pl.when(inside[d])(action)

    def remote(src, dst, sems, k, d):
        return pltpu.make_async_remote_copy(
            src_ref=src, dst_ref=dst, send_sem=sems[0].at[k], recv_sem=sems[1].at[k],
            device_id=device(*d), device_id_type=MESH,
        )

    barrier = pltpu.get_barrier_semaphore()
    def greet(d):
        return d, lambda: pl.semaphore_signal(barrier, inc=1, device_id=device(*d), device_id_type=MESH)

    each([greet(d) for d in DIRECTIONS])
    scalar_loads = (
        pltpu.make_async_copy(agg_hbm, agg, scalar_sem.at[0]),
        pltpu.make_async_copy(links_hbm, links, scalar_sem.at[1]),
    )
    p_loads, a_loads = [], []
    for c, (sx, sy) in enumerate(CORNERS):
        x, y = (sx + 1) // 2, (sy + 1) // 2
        p_loads.append(pltpu.make_async_copy(p_hbm.at[x, y], p_v.at[x, y], p_sem.at[c]))
        a_loads.append(pltpu.make_async_copy(a_hbm.at[x, y], a_v.at[x, y], a_sem.at[c]))
    for copy in (*scalar_loads, *p_loads):
        copy.start()

    even_row = (lax.broadcasted_iota(jnp.int32, (1, 128), 1) >= 64).astype(jnp.int32) == par
    even = (lax.broadcasted_iota(jnp.int32, (128, 128), 1) >= 64).astype(jnp.int32) == par
    top = jnp.full((64, 128), par, jnp.int32) == 0

    @pl.when(jnp.logical_not(interior))
    def _():
        for k, d in enumerate(DIRECTIONS):

            @pl.when(jnp.logical_not(inside[d]))
            def _():
                if k < 4:
                    face_in[k] = jnp.zeros((64, 896), BF16)
                else:
                    rest_in[k - 4] = jnp.zeros((64, 384), BF16)
                for c, (sx, sy) in enumerate(CORNERS):
                    if d == (sx, 0):
                        raw_x[c] = jnp.zeros((3, 128, 128), BF16)
                        first_in[c] = jnp.zeros((64, 256), BF16)
                    if d == (0, sy):
                        raw_y[c] = jnp.zeros((3, 128, 128), BF16)

    def place(x, y, z, fact):
        return FACTS * (4 * x + 2 * y + z) + fact

    for copy in scalar_loads:
        copy.wait()
    for c, (sx, sy) in enumerate(CORNERS):
        x, y = (sx + 1) // 2, (sy + 1) // 2
        ix, iy, ox, oy = slots(sx, sy)
        for z in range(2):
            mz = 6 if z == 0 else 5
            mine = agg[x, y, z]
            facts[place(x, y, z, 0)] = mine
            for fact, m, target in (
                (1, mz, agg[x, y, 1 - z]), (2, ix, agg[1 - x, y, z]), (3, iy, agg[x, 1 - y, z]), (4, ox, mine), (5, oy, mine)
            ):
                facts[place(x, y, z, fact)] = jnp.where(links[x, y, z, m - 1] == 1, target, NOWHERE)

    def pack(evens_first):
        for c, (sx, sy) in enumerate(CORNERS):
            x, y = (sx + 1) // 2, (sy + 1) // 2
            ix, iy, ox, oy = slots(sx, sy)
            p_loads[c].wait()
            for z in range(2):
                for j, (m, n) in enumerate(((0, 6 if z == 0 else 5), (ix, iy), (ox, oy))):
                    pair = [p_v[x, y, z, m], p_v[x, y, z, n]]
                    raw[c, j, 64 * z : 64 * z + 64, :] = jnp.concatenate(pair if evens_first else pair[::-1], axis=1)

    pl.when(par == 0)(lambda: pack(True))
    pl.when(par == 1)(lambda: pack(False))

    for copy in a_loads:
        copy.start()
    pl.semaphore_wait(barrier, sum(there.astype(jnp.int32) for there in inside.values()))

    facts_copies = {}
    for k, (dx, dy) in enumerate(DIRECTIONS):
        facts_copies[dx, dy] = remote(facts, facts_in.at[k], (facts_s, facts_r), k, (-dx, -dy))
    copies_x, copies_y = [], []
    for c, (sx, sy) in enumerate(CORNERS):
        copies_x.append(remote(raw.at[corner(-sx, sy)], raw_x.at[c], (raw_s, raw_r), c, (-sx, 0)))
        copies_y.append(remote(raw.at[corner(sx, -sy)], raw_y.at[c], (raw_s, raw_r), 4 + c, (0, -sy)))
    each(
        [((-dx, -dy), facts_copies[dx, dy].start) for dx, dy in CORNERS + FACES]
        + [((0, -sy), copies_y[c].start) for c, (sx, sy) in enumerate(CORNERS)]
        + [((-sx, 0), copies_x[c].start) for c, (sx, sy) in enumerate(CORNERS)]
    )

    for c, (sx, sy) in enumerate(CORNERS):
        x, y = (sx + 1) // 2, (sy + 1) // 2
        a_loads[c].wait()

        def block(z, m):
            value = a_v[x, y, z, m]
            if m == 0:
                return value
            return (value.astype(F32) * links[x, y, z, m - 1].astype(F32)).astype(BF16)

        mats[c, 0, 0:64, :] = jnp.concatenate([block(0, 0), block(0, 6)], axis=1)
        mats[c, 0, 64:128, :] = jnp.concatenate([block(1, 5), block(1, 0)], axis=1)
        zero = jnp.zeros((64, 64), BF16)
        for k, m in enumerate(slots(sx, sy)):
            mats[c, k + 1, 0:64, :] = jnp.concatenate([block(0, m), zero], axis=1)
            mats[c, k + 1, 64:128, :] = jnp.concatenate([zero, block(1, m)], axis=1)

    def told(d, x, y, z, fact):
        return jnp.where(inside[d], facts_in[DIRECTIONS.index(d), place(x, y, z, fact)], NOWHERE)

    def combine(source, target, names, flipped, origin, targets):
        def lane_ids(pair):
            first, second = (((mx + origin[0] + t[0]) * ny + my + origin[1] + t[1]) for t in pair)
            return jnp.where(even_row, second, first) if flipped else jnp.where(even_row, first, second)

        ids = [lane_ids(pair) for pair in names]
        swapped = [lane_ids(pair[::-1]) for pair in names]
        evens = jnp.logical_not(even_row) if flipped else even_row
        for z in range(2):
            rows = slice(64 * z, 64 * z + 64)
            boxes = targets(z)
            values = [source[j, rows, :].astype(F32) for j in range(3)]
            lanes = [jnp.where(evens, boxes[2 * j], boxes[2 * j + 1]) for j in range(3)]

            def picked(names, which):
                return sum(values[j] * (lanes[j] == names).astype(F32) for j in which)

            target[0, rows, :] = (
                picked(ids[0], (0, 1, 2)) + pltpu.roll(picked(swapped[0], (0, 1, 2)), 64, 1)
            ).astype(BF16)
            target[1, rows, :] = (picked(ids[1], (0, 2)) + pltpu.roll(picked(swapped[1], (0, 1)), 64, 1)).astype(BF16)
            target[2, rows, :] = picked(ids[2], (1,)).astype(BF16)

    each([(d, facts_copies[d].wait_recv) for d in FACES])
    for c, (sx, sy) in enumerate(CORNERS):
        x, y = (sx + 1) // 2, (sy + 1) // 2
        combine(
            raw.at[c], tiles.at[c], element_tiles(sx, sy), False, (0, 0),
            lambda z: [facts[place(x, y, z, fact)] for fact in range(4)]
            + [told((sx, 0), 1 - x, y, z, 4), told((0, sy), x, 1 - y, z, 5)],
        )

    for c, (sx, sy) in enumerate(CORNERS):
        blocks = {}
        for t, pair in enumerate(element_tiles(sx, sy)):
            turned = tiles[c, t].astype(F32).T
            blocks[pair[0]] = jnp.where(top, turned[0:64], turned[64:128]).astype(BF16)
            blocks[pair[1]] = jnp.where(top, turned[64:128], turned[0:64]).astype(BF16)
        ptd[c] = blocks[sx, sy]
        for r, offset in enumerate(FACES + ((0, 0),)):
            ptg[64 * r : 64 * r + 64, 128 * c : 128 * c + 128] = blocks[offset]

    def product(mat, ref, c):
        rows = dot(mat, jnp.concatenate([ref[c, 0], ref[c, 1], ref[c, 2]], axis=1))
        return rows[:, 0:128], rows[:, 128:256], rows[:, 256:384]

    nothing = jnp.zeros((128, 128), F32)
    for c, (sx, sy) in enumerate(CORNERS):
        s0, s1, s2 = product(mats[c, 0], tiles, c)
        x0, x1, x2 = product(mats[c, 1], tiles, corner(-sx, sy))
        y0, y1, y2 = product(mats[c, 2], tiles, corner(sx, -sy))
        im[c, 0] = s0 + jnp.where(even, x0 + y0, nothing)
        im[c, 1] = s1 + jnp.where(even, x2 + y1, x1 + y2)
        im[c, 2] = s2 + jnp.where(even, x1 + y2, x2 + y1)
        im[c, 3] = jnp.where(even, nothing, y0)
        im[c, 4] = jnp.where(even, nothing, x0)

    for jx in range(7):
        for jy in range(7):
            if abs(jx - 3) + abs(jy - 3) > 3:
                out[0, 0, jx, jy] = jnp.zeros((64, 64), BF16)

    each(
        [(d, facts_copies[d].wait_recv) for d in CORNERS]
        + [((sx, 0), copies_x[c].wait_recv) for c, (sx, sy) in enumerate(CORNERS)]
    )
    for c, (sx, sy) in enumerate(CORNERS):
        x, y = (sx + 1) // 2, (sy + 1) // 2
        combine(
            raw_x.at[c], tiles_x.at[c], element_tiles(-sx, sy), False, (sx, 0),
            lambda z: [told((sx, 0), 1 - x, y, z, fact) for fact in range(4)]
            + [facts[place(x, y, z, 4)], told((sx, sy), 1 - x, 1 - y, z, 5)],
        )
    for c in range(4):
        x0, x1, x2 = product(mats[c, 3], tiles_x, c)
        im[c, 0] += x1
        im[c, 1] += x0
        im[c, 3] += x2
    for c in range(4):
        first = jnp.concatenate([im[c, 2].astype(BF16), im[c, 3].astype(BF16)], axis=1)
        first_out[c] = dot(ptd[c], first).astype(BF16)
    first_copies = [
        remote(first_out.at[corner(-sx, sy)], first_in.at[c], (first_s, first_r), c, (-sx, 0))
        for c, (sx, sy) in enumerate(CORNERS)
    ]
    each([((-sx, 0), first_copies[c].start) for c, (sx, sy) in enumerate(CORNERS)])

    rest_copies = [
        remote(rest_out.at[corner(-sx, -sy)], rest_in.at[c], (rest_s, rest_r), c, (-sx, -sy))
        for c, (sx, sy) in enumerate(CORNERS)
    ]
    for group in ((0,), (1,), (2,), (3,)):
        each([((0, CORNERS[c][1]), copies_y[c].wait_recv) for c in group])
        for c in group:
            sx, sy = CORNERS[c]
            x, y = (sx + 1) // 2, (sy + 1) // 2
            combine(
                raw_y.at[c], tiles_y.at[c], element_tiles(sx, -sy), True, (0, sy),
                lambda z: [told((0, sy), x, 1 - y, z, fact) for fact in range(4)]
                + [told((sx, sy), 1 - x, 1 - y, z, 4), facts[place(x, y, z, 5)]],
            )
        for c in group:
            sx, sy = CORNERS[c]
            y0, y1, y2 = product(mats[c, 4], tiles_y, c)
            image = [im[c, 0] + y1, im[c, 1] + y0, im[c, 2], im[c, 3], im[c, 4] + y2]
            rest = jnp.concatenate([image[0].astype(BF16), image[1].astype(BF16), image[4].astype(BF16)], axis=1)
            rest_out[c] = dot(ptd[c], rest).astype(BF16)
            names = image_tiles(sx, sy)
            at_even = {pair[0]: i for i, pair in enumerate(names)}
            at_odd = {pair[1]: i for i, pair in enumerate(names)}
            for g, (e, o) in enumerate(PAIRS):
                evens = image[at_even[e]] if e in at_even else nothing
                odds = image[at_odd[o]] if o in at_odd else nothing
                imw[128 * c : 128 * c + 128, 128 * g : 128 * g + 128] = jnp.where(even, evens, odds).astype(BF16)
        each([(CORNERS[c], rest_copies[3 - c].start) for c in group])

    each([((sx, 0), first_copies[c].wait_recv) for c, (sx, sy) in enumerate(CORNERS)])
    passed = {}
    for c, (sx, sy) in enumerate(CORNERS):
        for i, pair in enumerate(image_tiles(-sx, sy)[2:4]):
            tile = first_in[c, :, 128 * i : 128 * i + 128].astype(F32)
            for side, offset in enumerate(pair):
                g = (EVENS, ODDS)[side].index(add(offset, (sx, 0)))
                key = (sy, g, side)
                passed[key] = tile if key not in passed else passed[key] + tile

    def with_passed(tile, sy, g):
        halves = [passed.get((sy, g, side)) for side in range(2)]
        if halves == [None, None]:
            return tile
        halves = [nothing[0:64] if half is None else half for half in halves]
        return tile + jnp.where(even[0:64], *halves)

    wide = imw[...]
    face_copies = [
        remote(face_out.at[FACES.index((-dx, -dy))], face_in.at[k], (face_s, face_r), k, (-dx, -dy))
        for k, (dx, dy) in enumerate(FACES)
    ]
    for first in (2, 0):
        rows = dot(ptg[64 * first : 64 * first + 128, :], wide)
        for k in (first, first + 1):
            for g in range(len(PAIRS)):
                tile = rows[64 * (k - first) : 64 * (k - first) + 64, 128 * g : 128 * g + 128]
                if first == 2:
                    tile = with_passed(tile, FACES[k][1], g)
                face_out[k, :, 128 * g : 128 * g + 128] = tile.astype(BF16)
        each([((-FACES[k][0], -FACES[k][1]), face_copies[k].start) for k in (first, first + 1)])

    offsets = [(dx, dy) for dx in range(-3, 4) for dy in range(-3, 4) if abs(dx) + abs(dy) <= 3]
    at = {offset: i for i, offset in enumerate(offsets)}

    def tiles_of(ref, names, d):
        return [
            (add(offset, d), ref, g) for g, pair in enumerate(names) for offset in pair if offset is not None
        ]

    own = dot(ptg[256:320, :], wide)
    mine = {offset: g for g, pair in enumerate(PAIRS) for offset in pair if offset is not None}
    early = [source for k in (0, 1) for source in tiles_of(face_in.at[k], PAIRS, FACES[k])]
    late = []
    for c, (sx, sy) in enumerate(CORNERS):
        names = image_tiles(-sx, -sy)
        late.extend(tiles_of(rest_in.at[c], (names[0], names[1], names[4]), (sx, sy)))

    def gathered(total, offset, sources):
        for name, ref, g in sources:
            if name == offset:
                tile = ref[:, 128 * g : 128 * g + 128].astype(F32)
                total = tile if total is None else total + tile
        return jnp.zeros((64, 128), F32) if total is None else total

    each([(FACES[k], face_copies[k].wait_recv) for k in (0, 1)])
    for offset in offsets:
        g = mine.get(offset)
        acc[at[offset]] = gathered(None if g is None else own[:, 128 * g : 128 * g + 128], offset, early)
    each(
        [((-dx, -dy), facts_copies[dx, dy].wait_send) for dx, dy in DIRECTIONS]
        + [((-sx, 0), copies_x[c].wait_send) for c, (sx, sy) in enumerate(CORNERS)]
        + [((0, -sy), copies_y[c].wait_send) for c, (sx, sy) in enumerate(CORNERS)]
        + [((-sx, 0), first_copies[c].wait_send) for c, (sx, sy) in enumerate(CORNERS)]
        + [((sx, sy), rest_copies[c].wait_recv) for c, (sx, sy) in enumerate(CORNERS)]
    )

    def finish(evens_first):
        def on_left(value, offset):
            return value if (offset[1] % 2 == 0) == evens_first else pltpu.roll(value, 64, 1)

        def put(offset, value):
            out[0, 0, offset[0] + 3, offset[1] + 3] = value[:, 0:64].astype(BF16)

        last = {}
        for k in (2, 3):
            for g, pair in enumerate(PAIRS):
                for offset in pair:
                    if offset is not None:
                        last.setdefault(add(offset, FACES[k]), []).append((k, g))
        for offset in offsets:
            value = on_left(gathered(acc[at[offset]], offset, late), offset)
            if offset in last:
                acc[at[offset]] = value
            else:
                put(offset, value)
        each(
            [((-sx, -sy), rest_copies[c].wait_send) for c, (sx, sy) in enumerate(CORNERS)]
            + [((-FACES[k][0], -FACES[k][1]), face_copies[k].wait_send) for k in (0, 1)]
            + [(FACES[k], face_copies[k].wait_recv) for k in (2, 3)]
        )
        for offset in offsets:
            if offset in last:
                value = acc[at[offset]]
                for k, g in last[offset]:
                    value += on_left(face_in[k, :, 128 * g : 128 * g + 128], offset).astype(F32)
                put(offset, value)

    pl.when(par == 0)(lambda: finish(True))
    pl.when(par == 1)(lambda: finish(False))

    each([((-FACES[k][0], -FACES[k][1]), face_copies[k].wait_send) for k in (2, 3)])


def per_device(fine_matrix, prolongator, aggregate, face_links):
    nx, ny = lax.axis_size("sx"), lax.axis_size("sy")
    dma = pltpu.SemaphoreType.DMA
    return pl.pallas_call(
        functools.partial(kernel, nx, ny),
        out_shape=jax.ShapeDtypeStruct((1, 1, 7, 7, 64, 64), BF16),
        in_specs=[pl.BlockSpec(memory_space=pl.ANY)] * 4,
        out_specs=pl.BlockSpec(memory_space=pltpu.VMEM),
        scratch_shapes=[
            pltpu.VMEM((2, 2, 2, 7, 64, 64), BF16),
            pltpu.VMEM((2, 2, 2, 7, 64, 64), BF16),
            pltpu.SMEM((2, 2, 2), jnp.int32),
            pltpu.SMEM((2, 2, 2, 6), jnp.int32),
            pltpu.SMEM((64,), jnp.int32),
            pltpu.SMEM((8, 64), jnp.int32),
            *[pltpu.VMEM((4, 3, 128, 128), BF16)] * 6,
            pltpu.VMEM((4, 5, 128, 128), BF16),
            pltpu.VMEM((4, 5, 128, 128), F32),
            pltpu.VMEM((320, 512), BF16),
            pltpu.VMEM((4, 64, 128), BF16),
            pltpu.VMEM((512, 896), BF16),
            *[pltpu.VMEM((4, 64, 896), BF16)] * 2,
            *[pltpu.VMEM((4, 64, 256), BF16)] * 2,
            *[pltpu.VMEM((4, 64, 384), BF16)] * 2,
            pltpu.VMEM((25, 64, 128), F32),
            dma((2,)),
            dma((4,)),
            dma((4,)),
            *[dma((8,))] * 4,
            *[dma((4,))] * 6,
        ],
        compiler_params=pltpu.CompilerParams(
            collective_id=0, has_side_effects=True, vmem_limit_bytes=32 * 1024 * 1024
        ),
        name="galerkin",
    )(*(pltpu.with_memory_space_constraint(v, pltpu.HBM) for v in (fine_matrix, prolongator, aggregate, face_links)))


def solution(mesh):
    return jax.shard_map(
        per_device,
        mesh=mesh,
        in_specs=(
            P("sx", "sy", None, None, None, None),
            P("sx", "sy", None, None, None, None),
            P("sx", "sy", None),
            P("sx", "sy", None, None),
        ),
        out_specs=P("sx", "sy", None, None, None, None),
        check_vma=False,
    )
```

```python
import functools

import jax
import jax.numpy as jnp
from jax import lax
from jax.experimental import pallas as pl
from jax.experimental.pallas import tpu as pltpu
from jax.sharding import PartitionSpec as P

MESH = pl.DeviceIdType.MESH
F32 = jnp.float32
BF16 = jnp.bfloat16

CORNERS = ((-1, -1), (-1, 1), (1, -1), (1, 1))
FACES = ((-1, 0), (1, 0), (0, -1), (0, 1))
DIRECTIONS = FACES + CORNERS
NOWHERE = -1000000
FACTS = 6

EVENS = ((0, 0), (-1, 0), (1, 0), (-2, 0), (2, 0), (0, -2), (0, 2))
ODDS = ((0, -1), (0, 1), (-1, -1), (-1, 1), (1, -1), (1, 1), None)
PAIRS = tuple(zip(EVENS, ODDS))


def corner(sx, sy):
    return (2 if sx > 0 else 0) + (1 if sy > 0 else 0)


def element_tiles(sx, sy):
    return (((0, 0), (sx, sy)), ((sx, 0), (0, sy)), ((-sx, 0), (0, -sy)))


def image_tiles(sx, sy):
    return element_tiles(sx, sy) + (((2 * sx, 0), (sx, -sy)), ((0, 2 * sy), (-sx, sy)))


def slots(sx, sy):
    return (2 if sx < 0 else 1), (4 if sy < 0 else 3), (1 if sx < 0 else 2), (3 if sy < 0 else 4)


def add(u, v):
    return (u[0] + v[0], u[1] + v[1])


def dot(a, b):
    return jnp.dot(a, b, preferred_element_type=F32)


def kernel(
    nx, ny, a_hbm, p_hbm, agg_hbm, links_hbm, out,
    a_v, p_v, agg, links, facts, facts_in, raw, raw_x, raw_y, tiles, tiles_x, tiles_y, mats, im, ptg, ptd, imw,
    face_out, face_in, first_out, first_in, rest_out, rest_in, acc,
    scalar_sem, p_sem, a_sem, facts_s, facts_r, raw_s, raw_r, face_s, face_r, first_s, first_r, rest_s, rest_r,
):
    mx, my = lax.axis_index("sx"), lax.axis_index("sy")
    par = lax.rem(my, 2)

    def device(dx, dy):
        return (lax.rem(mx + dx + nx, nx), lax.rem(my + dy + ny, ny))

    inside = {(-1, 0): mx > 0, (1, 0): mx < nx - 1, (0, -1): my > 0, (0, 1): my < ny - 1}
    for sx, sy in CORNERS:
        inside[sx, sy] = jnp.logical_and(inside[sx, 0], inside[0, sy])

    interior = jnp.logical_and(
        jnp.logical_and(inside[-1, 0], inside[1, 0]), jnp.logical_and(inside[0, -1], inside[0, 1])
    )

    def each(actions):
        @pl.when(interior)
        def _():
            for _, action in actions:
                action()

        @pl.when(jnp.logical_not(interior))
        def _():
            for d, action in actions:
                pl.when(inside[d])(action)

    def remote(src, dst, sems, k, d):
        return pltpu.make_async_remote_copy(
            src_ref=src, dst_ref=dst, send_sem=sems[0].at[k], recv_sem=sems[1].at[k],
            device_id=device(*d), device_id_type=MESH,
        )

    barrier = pltpu.get_barrier_semaphore()
    def greet(d):
        return d, lambda: pl.semaphore_signal(barrier, inc=1, device_id=device(*d), device_id_type=MESH)

    each([greet(d) for d in DIRECTIONS])
    scalar_loads = (
        pltpu.make_async_copy(agg_hbm, agg, scalar_sem.at[0]),
        pltpu.make_async_copy(links_hbm, links, scalar_sem.at[1]),
    )
    p_loads, a_loads = [], []
    for c, (sx, sy) in enumerate(CORNERS):
        x, y = (sx + 1) // 2, (sy + 1) // 2
        for k, (z, first, count) in enumerate(((0, 0, 5), (0, 6, 1), (1, 0, 6))):
            blocks = (x, y, z, pl.ds(first, count))
            p_loads.append(pltpu.make_async_copy(p_hbm.at[blocks], p_v.at[blocks], p_sem.at[3 * c + k]))
        a_loads.append(pltpu.make_async_copy(a_hbm.at[x, y], a_v.at[x, y], a_sem.at[c]))
    for copy in (*scalar_loads, *p_loads):
        copy.start()

    even_row = (lax.broadcasted_iota(jnp.int32, (1, 128), 1) >= 64).astype(jnp.int32) == par
    even = (lax.broadcasted_iota(jnp.int32, (128, 128), 1) >= 64).astype(jnp.int32) == par
    top = jnp.full((64, 128), par, jnp.int32) == 0

    @pl.when(jnp.logical_not(interior))
    def _():
        for k, d in enumerate(DIRECTIONS):

            @pl.when(jnp.logical_not(inside[d]))
            def _():
                if k < 4:
                    face_in[k] = jnp.zeros((64, 896), BF16)
                else:
                    rest_in[k - 4] = jnp.zeros((64, 384), BF16)
                for c, (sx, sy) in enumerate(CORNERS):
                    if d == (sx, 0):
                        raw_x[c] = jnp.zeros((3, 128, 128), BF16)
                        first_in[c] = jnp.zeros((64, 256), BF16)
                    if d == (0, sy):
                        raw_y[c] = jnp.zeros((3, 128, 128), BF16)

    def place(x, y, z, fact):
        return FACTS * (4 * x + 2 * y + z) + fact

    for copy in scalar_loads:
        copy.wait()
    for c, (sx, sy) in enumerate(CORNERS):
        x, y = (sx + 1) // 2, (sy + 1) // 2
        ix, iy, ox, oy = slots(sx, sy)
        for z in range(2):
            mz = 6 if z == 0 else 5
            mine = agg[x, y, z]
            facts[place(x, y, z, 0)] = mine
            for fact, m, target in (
                (1, mz, agg[x, y, 1 - z]), (2, ix, agg[1 - x, y, z]), (3, iy, agg[x, 1 - y, z]), (4, ox, mine), (5, oy, mine)
            ):
                facts[place(x, y, z, fact)] = jnp.where(links[x, y, z, m - 1] == 1, target, NOWHERE)

    def pack(evens_first):
        for c, (sx, sy) in enumerate(CORNERS):
            x, y = (sx + 1) // 2, (sy + 1) // 2
            ix, iy, ox, oy = slots(sx, sy)
            for copy in p_loads[3 * c : 3 * c + 3]:
                copy.wait()
            for z in range(2):
                for j, (m, n) in enumerate(((0, 6 if z == 0 else 5), (ix, iy), (ox, oy))):
                    pair = [p_v[x, y, z, m], p_v[x, y, z, n]]
                    raw[c, j, 64 * z : 64 * z + 64, :] = jnp.concatenate(pair if evens_first else pair[::-1], axis=1)

    pl.when(par == 0)(lambda: pack(True))
    pl.when(par == 1)(lambda: pack(False))

    for copy in a_loads:
        copy.start()
    pl.semaphore_wait(barrier, sum(there.astype(jnp.int32) for there in inside.values()))

    facts_copies = {}
    for k, (dx, dy) in enumerate(DIRECTIONS):
        facts_copies[dx, dy] = remote(facts, facts_in.at[k], (facts_s, facts_r), k, (-dx, -dy))
    copies_x, copies_y = [], []
    for c, (sx, sy) in enumerate(CORNERS):
        copies_x.append(remote(raw.at[corner(-sx, sy)], raw_x.at[c], (raw_s, raw_r), c, (-sx, 0)))
        copies_y.append(remote(raw.at[corner(sx, -sy)], raw_y.at[c], (raw_s, raw_r), 4 + c, (0, -sy)))
    each(
        [((-dx, -dy), facts_copies[dx, dy].start) for dx, dy in CORNERS + FACES]
        + [((0, -CORNERS[c][1]), copies_y[c].start) for c in (0, 1)]
        + [((-sx, 0), copies_x[c].start) for c, (sx, sy) in enumerate(CORNERS)]
        + [((0, -CORNERS[c][1]), copies_y[c].start) for c in (2, 3)]
    )

    for c, (sx, sy) in enumerate(CORNERS):
        x, y = (sx + 1) // 2, (sy + 1) // 2
        a_loads[c].wait()

        def block(z, m):
            value = a_v[x, y, z, m]
            if m == 0:
                return value
            return (value.astype(F32) * links[x, y, z, m - 1].astype(F32)).astype(BF16)

        mats[c, 0, 0:64, :] = jnp.concatenate([block(0, 0), block(0, 6)], axis=1)
        mats[c, 0, 64:128, :] = jnp.concatenate([block(1, 5), block(1, 0)], axis=1)
        zero = jnp.zeros((64, 64), BF16)
        for k, m in enumerate(slots(sx, sy)):
            mats[c, k + 1, 0:64, :] = jnp.concatenate([block(0, m), zero], axis=1)
            mats[c, k + 1, 64:128, :] = jnp.concatenate([zero, block(1, m)], axis=1)

    def told(d, x, y, z, fact):
        return jnp.where(inside[d], facts_in[DIRECTIONS.index(d), place(x, y, z, fact)], NOWHERE)

    def combine(source, target, names, flipped, origin, targets):
        def lane_ids(pair):
            first, second = (((mx + origin[0] + t[0]) * ny + my + origin[1] + t[1]) for t in pair)
            return jnp.where(even_row, second, first) if flipped else jnp.where(even_row, first, second)

        ids = [lane_ids(pair) for pair in names]
        swapped = [lane_ids(pair[::-1]) for pair in names]
        evens = jnp.logical_not(even_row) if flipped else even_row
        for z in range(2):
            rows = slice(64 * z, 64 * z + 64)
            boxes = targets(z)
            values = [source[j, rows, :].astype(F32) for j in range(3)]
            lanes = [jnp.where(evens, boxes[2 * j], boxes[2 * j + 1]) for j in range(3)]

            def picked(names, which):
                return sum(values[j] * (lanes[j] == names).astype(F32) for j in which)

            target[0, rows, :] = (
                picked(ids[0], (0, 1, 2)) + pltpu.roll(picked(swapped[0], (0, 1, 2)), 64, 1)
            ).astype(BF16)
            target[1, rows, :] = (picked(ids[1], (0, 2)) + pltpu.roll(picked(swapped[1], (0, 1)), 64, 1)).astype(BF16)
            target[2, rows, :] = picked(ids[2], (1,)).astype(BF16)

    each([(d, facts_copies[d].wait_recv) for d in FACES])
    for c, (sx, sy) in enumerate(CORNERS):
        x, y = (sx + 1) // 2, (sy + 1) // 2
        combine(
            raw.at[c], tiles.at[c], element_tiles(sx, sy), False, (0, 0),
            lambda z: [facts[place(x, y, z, fact)] for fact in range(4)]
            + [told((sx, 0), 1 - x, y, z, 4), told((0, sy), x, 1 - y, z, 5)],
        )

    for c, (sx, sy) in enumerate(CORNERS):
        blocks = {}
        for t, pair in enumerate(element_tiles(sx, sy)):
            turned = tiles[c, t].astype(F32).T
            blocks[pair[0]] = jnp.where(top, turned[0:64], turned[64:128]).astype(BF16)
            blocks[pair[1]] = jnp.where(top, turned[64:128], turned[0:64]).astype(BF16)
        ptd[c] = blocks[sx, sy]
        for r, offset in enumerate(FACES + ((0, 0),)):
            ptg[64 * r : 64 * r + 64, 128 * c : 128 * c + 128] = blocks[offset]

    def product(mat, ref, c):
        rows = dot(mat, jnp.concatenate([ref[c, 0], ref[c, 1], ref[c, 2]], axis=1))
        return rows[:, 0:128], rows[:, 128:256], rows[:, 256:384]

    nothing = jnp.zeros((128, 128), F32)
    for c, (sx, sy) in enumerate(CORNERS):
        s0, s1, s2 = product(mats[c, 0], tiles, c)
        x0, x1, x2 = product(mats[c, 1], tiles, corner(-sx, sy))
        y0, y1, y2 = product(mats[c, 2], tiles, corner(sx, -sy))
        im[c, 0] = s0 + jnp.where(even, x0 + y0, nothing)
        im[c, 1] = s1 + jnp.where(even, x2 + y1, x1 + y2)
        im[c, 2] = s2 + jnp.where(even, x1 + y2, x2 + y1)
        im[c, 3] = jnp.where(even, nothing, y0)
        im[c, 4] = jnp.where(even, nothing, x0)

    for jx in range(7):
        for jy in range(7):
            if abs(jx - 3) + abs(jy - 3) > 3:
                out[0, 0, jx, jy] = jnp.zeros((64, 64), BF16)

    each(
        [(d, facts_copies[d].wait_recv) for d in CORNERS]
        + [((sx, 0), copies_x[c].wait_recv) for c, (sx, sy) in enumerate(CORNERS)]
    )
    for c, (sx, sy) in enumerate(CORNERS):
        x, y = (sx + 1) // 2, (sy + 1) // 2
        combine(
            raw_x.at[c], tiles_x.at[c], element_tiles(-sx, sy), False, (sx, 0),
            lambda z: [told((sx, 0), 1 - x, y, z, fact) for fact in range(4)]
            + [facts[place(x, y, z, 4)], told((sx, sy), 1 - x, 1 - y, z, 5)],
        )
    for c in range(4):
        x0, x1, x2 = product(mats[c, 3], tiles_x, c)
        im[c, 0] += x1
        im[c, 1] += x0
        im[c, 3] += x2
    for c in range(4):
        first = jnp.concatenate([im[c, 2].astype(BF16), im[c, 3].astype(BF16)], axis=1)
        first_out[c] = dot(ptd[c], first).astype(BF16)
    first_copies = [
        remote(first_out.at[corner(-sx, sy)], first_in.at[c], (first_s, first_r), c, (-sx, 0))
        for c, (sx, sy) in enumerate(CORNERS)
    ]
    each([((-sx, 0), first_copies[c].start) for c, (sx, sy) in enumerate(CORNERS)])

    rest_copies = [
        remote(rest_out.at[corner(-sx, -sy)], rest_in.at[c], (rest_s, rest_r), c, (-sx, -sy))
        for c, (sx, sy) in enumerate(CORNERS)
    ]
    for group in ((0,), (1,), (2,), (3,)):
        each([((0, CORNERS[c][1]), copies_y[c].wait_recv) for c in group])
        for c in group:
            sx, sy = CORNERS[c]
            x, y = (sx + 1) // 2, (sy + 1) // 2
            combine(
                raw_y.at[c], tiles_y.at[c], element_tiles(sx, -sy), True, (0, sy),
                lambda z: [told((0, sy), x, 1 - y, z, fact) for fact in range(4)]
                + [told((sx, sy), 1 - x, 1 - y, z, 4), facts[place(x, y, z, 5)]],
            )
        for c in group:
            sx, sy = CORNERS[c]
            y0, y1, y2 = product(mats[c, 4], tiles_y, c)
            image = [im[c, 0] + y1, im[c, 1] + y0, im[c, 2], im[c, 3], im[c, 4] + y2]
            rest = jnp.concatenate([image[0].astype(BF16), image[1].astype(BF16), image[4].astype(BF16)], axis=1)
            rest_out[c] = dot(ptd[c], rest).astype(BF16)
            names = image_tiles(sx, sy)
            at_even = {pair[0]: i for i, pair in enumerate(names)}
            at_odd = {pair[1]: i for i, pair in enumerate(names)}
            for g, (e, o) in enumerate(PAIRS):
                evens = image[at_even[e]] if e in at_even else nothing
                odds = image[at_odd[o]] if o in at_odd else nothing
                imw[128 * c : 128 * c + 128, 128 * g : 128 * g + 128] = jnp.where(even, evens, odds).astype(BF16)
        each([(CORNERS[c], rest_copies[3 - c].start) for c in group])

    each([((sx, 0), first_copies[c].wait_recv) for c, (sx, sy) in enumerate(CORNERS)])
    passed = {}
    for c, (sx, sy) in enumerate(CORNERS):
        for i, pair in enumerate(image_tiles(-sx, sy)[2:4]):
            tile = first_in[c, :, 128 * i : 128 * i + 128].astype(F32)
            for side, offset in enumerate(pair):
                g = (EVENS, ODDS)[side].index(add(offset, (sx, 0)))
                key = (sy, g, side)
                passed[key] = tile if key not in passed else passed[key] + tile

    def with_passed(tile, sy, g):
        halves = [passed.get((sy, g, side)) for side in range(2)]
        if halves == [None, None]:
            return tile
        halves = [nothing[0:64] if half is None else half for half in halves]
        return tile + jnp.where(even[0:64], *halves)

    wide = imw[...]
    face_copies = [
        remote(face_out.at[FACES.index((-dx, -dy))], face_in.at[k], (face_s, face_r), k, (-dx, -dy))
        for k, (dx, dy) in enumerate(FACES)
    ]
    for first in (2, 0):
        rows = dot(ptg[64 * first : 64 * first + 128, :], wide)
        for k in (first, first + 1):
            for g in range(len(PAIRS)):
                tile = rows[64 * (k - first) : 64 * (k - first) + 64, 128 * g : 128 * g + 128]
                if first == 2:
                    tile = with_passed(tile, FACES[k][1], g)
                face_out[k, :, 128 * g : 128 * g + 128] = tile.astype(BF16)
        each([((-FACES[k][0], -FACES[k][1]), face_copies[k].start) for k in (first, first + 1)])

    offsets = [(dx, dy) for dx in range(-3, 4) for dy in range(-3, 4) if abs(dx) + abs(dy) <= 3]
    at = {offset: i for i, offset in enumerate(offsets)}

    def tiles_of(ref, names, d):
        return [
            (add(offset, d), ref, g) for g, pair in enumerate(names) for offset in pair if offset is not None
        ]

    own = dot(ptg[256:320, :], wide)
    mine = {offset: g for g, pair in enumerate(PAIRS) for offset in pair if offset is not None}
    early = [source for k in (0, 1) for source in tiles_of(face_in.at[k], PAIRS, FACES[k])]
    late = []
    for c, (sx, sy) in enumerate(CORNERS):
        names = image_tiles(-sx, -sy)
        late.extend(tiles_of(rest_in.at[c], (names[0], names[1], names[4]), (sx, sy)))

    def gathered(total, offset, sources):
        for name, ref, g in sources:
            if name == offset:
                tile = ref[:, 128 * g : 128 * g + 128].astype(F32)
                total = tile if total is None else total + tile
        return jnp.zeros((64, 128), F32) if total is None else total

    each([(FACES[k], face_copies[k].wait_recv) for k in (0, 1)])
    for offset in offsets:
        g = mine.get(offset)
        acc[at[offset]] = gathered(None if g is None else own[:, 128 * g : 128 * g + 128], offset, early)
    each(
        [((-dx, -dy), facts_copies[dx, dy].wait_send) for dx, dy in DIRECTIONS]
        + [((-sx, 0), copies_x[c].wait_send) for c, (sx, sy) in enumerate(CORNERS)]
        + [((0, -sy), copies_y[c].wait_send) for c, (sx, sy) in enumerate(CORNERS)]
        + [((-sx, 0), first_copies[c].wait_send) for c, (sx, sy) in enumerate(CORNERS)]
        + [((sx, sy), rest_copies[c].wait_recv) for c, (sx, sy) in enumerate(CORNERS)]
    )

    def finish(evens_first):
        def on_left(value, offset):
            return value if (offset[1] % 2 == 0) == evens_first else pltpu.roll(value, 64, 1)

        def put(offset, value):
            out[0, 0, offset[0] + 3, offset[1] + 3] = value[:, 0:64].astype(BF16)

        last = {}
        for k in (2, 3):
            for g, pair in enumerate(PAIRS):
                for offset in pair:
                    if offset is not None:
                        last.setdefault(add(offset, FACES[k]), []).append((k, g))
        for offset in offsets:
            value = on_left(gathered(acc[at[offset]], offset, late), offset)
            if offset in last:
                acc[at[offset]] = value
            else:
                put(offset, value)
        each(
            [((-sx, -sy), rest_copies[c].wait_send) for c, (sx, sy) in enumerate(CORNERS)]
            + [((-FACES[k][0], -FACES[k][1]), face_copies[k].wait_send) for k in (0, 1)]
            + [(FACES[k], face_copies[k].wait_recv) for k in (2, 3)]
        )
        for offset in offsets:
            if offset in last:
                value = acc[at[offset]]
                for k, g in last[offset]:
                    value += on_left(face_in[k, :, 128 * g : 128 * g + 128], offset).astype(F32)
                put(offset, value)

    pl.when(par == 0)(lambda: finish(True))
    pl.when(par == 1)(lambda: finish(False))

    each([((-FACES[k][0], -FACES[k][1]), face_copies[k].wait_send) for k in (2, 3)])


def per_device(fine_matrix, prolongator, aggregate, face_links):
    nx, ny = lax.axis_size("sx"), lax.axis_size("sy")
    dma = pltpu.SemaphoreType.DMA
    return pl.pallas_call(
        functools.partial(kernel, nx, ny),
        out_shape=jax.ShapeDtypeStruct((1, 1, 7, 7, 64, 64), BF16),
        in_specs=[pl.BlockSpec(memory_space=pl.ANY)] * 4,
        out_specs=pl.BlockSpec(memory_space=pltpu.VMEM),
        scratch_shapes=[
            pltpu.VMEM((2, 2, 2, 7, 64, 64), BF16),
            pltpu.VMEM((2, 2, 2, 7, 64, 64), BF16),
            pltpu.SMEM((2, 2, 2), jnp.int32),
            pltpu.SMEM((2, 2, 2, 6), jnp.int32),
            pltpu.SMEM((64,), jnp.int32),
            pltpu.SMEM((8, 64), jnp.int32),
            *[pltpu.VMEM((4, 3, 128, 128), BF16)] * 6,
            pltpu.VMEM((4, 5, 128, 128), BF16),
            pltpu.VMEM((4, 5, 128, 128), F32),
            pltpu.VMEM((320, 512), BF16),
            pltpu.VMEM((4, 64, 128), BF16),
            pltpu.VMEM((512, 896), BF16),
            *[pltpu.VMEM((4, 64, 896), BF16)] * 2,
            *[pltpu.VMEM((4, 64, 256), BF16)] * 2,
            *[pltpu.VMEM((4, 64, 384), BF16)] * 2,
            pltpu.VMEM((25, 64, 128), F32),
            dma((2,)),
            dma((12,)),
            dma((4,)),
            *[dma((8,))] * 4,
            *[dma((4,))] * 6,
        ],
        compiler_params=pltpu.CompilerParams(
            collective_id=0, has_side_effects=True, vmem_limit_bytes=32 * 1024 * 1024
        ),
        name="galerkin",
    )(*(pltpu.with_memory_space_constraint(v, pltpu.HBM) for v in (fine_matrix, prolongator, aggregate, face_links)))


def solution(mesh):
    return jax.shard_map(
        per_device,
        mesh=mesh,
        in_specs=(
            P("sx", "sy", None, None, None, None),
            P("sx", "sy", None, None, None, None),
            P("sx", "sy", None),
            P("sx", "sy", None, None),
        ),
        out_specs=P("sx", "sy", None, None, None, None),
        check_vma=False,
    )
```
